128 devices in a mesh: row: 8 (over y_lo, z), col: 16 (over y_hi, x, core).
Axes of the slice: x: 4, y: 4 (y_hi: 2, y_lo: 2; y = y_hi * 2 + y_lo), z: 4, core: 2. Of those that a mesh axis runs over, the one named last changes fastest.
Arguments:
- block_values: bfloat16 [32, 16, 256, 256], P('row', 'col'), may hold values from -0.625 to 0.625
- block_columns: int32 [32, 16], P('row', 'col'), may hold values from 0 to 1
- block_live: int32 [32, 16], P('row', 'col'), may hold values 0 or 1
Outputs:
- updated: bfloat16 [32, 16, 256, 256], P('row', 'col')
The draws below stay inside these ranges and needn't reach their ends.
All inputs are finite; a program needn't handle non-finite values. No bound on the sum of `block_live` on one device may be relied on, other than what follows from the above.
Results may differ from the reference program's by a relative error of at most 0.0048.
Values may be sent and summed in bfloat16 or wider, within the bound.
A program may use at most 128 MiB of HBM per device.

```python
import jax
import jax.numpy as jnp
from jax import lax

BS = 256
NB = 32
CB = 2
N_COL = 16


def plant(array, key, smallest, high):
    dims = array.shape
    spot = [jax.random.randint(jax.random.fold_in(key, axis), (), 0, dims[axis]) for axis in range(len(dims))]
    array = array.at[tuple(spot)].set(smallest)
    longest = dims.index(max(dims))
    spot[longest] = (spot[longest] + 1) % dims[longest]
    return array.at[tuple(spot)].set(high)


def level_of(key, extent, split, smallest, top_value):
    def one(axis_at, parts):
        draws = jax.random.uniform(jax.random.fold_in(jax.random.fold_in(key, 6), axis_at), (parts,), jnp.float32, smallest / len(split), top_value / len(split))
        return jnp.repeat(jnp.exp(draws), extent[axis_at] // parts).reshape((-1,) + (1,) * (len(extent) - axis_at - 1))

    factor_of = one(*split[0])
    for cut in split[1:]:
        factor_of = factor_of * one(*cut)
    return factor_of


def normal_values(stream_key, shape, spread, reach, split=(), kind=jnp.bfloat16):
    gain = level_of(stream_key, shape, split, -0.22, 0.18) if split else 1.0
    values = jax.random.normal(stream_key, shape, jnp.float32) * spread * gain
    return jnp.minimum(jnp.maximum(values, -reach), reach).astype(kind)


def setup_inputs(seed: int = 0) -> dict:
    streams_of = jax.random.split(jax.random.key(seed), 4)
    block_values = normal_values(streams_of[0], (NB, N_COL, BS, BS), (BS // 3) ** -0.5, 0.625, ((0, 8), (1, 16)))
    block_columns = plant(jax.random.randint(streams_of[1], (NB, N_COL), 0, CB), jax.random.fold_in(streams_of[1], 1), 0, CB - 1).astype(jnp.int32)
    block_live = plant((jax.random.randint(streams_of[2], (NB, N_COL), 0, 4) < 3).astype(jnp.int32), jax.random.fold_in(streams_of[2], 1), 0, 1)
    return {"block_values": block_values, "block_columns": block_columns, "block_live": block_live}


def filtered_product(left_side, right_side, block_columns, block_live):
    offsets = jnp.arange(N_COL, dtype=jnp.int32) * CB

    def one_row(row_index):
        left_blocks = left_side[row_index]
        own_columns = block_columns[row_index]
        source_rows = (offsets + own_columns).astype(jnp.int32)
        right_blocks = right_side[source_rows]
        matches = (block_columns[source_rows] == own_columns[None, :]) & (block_live[row_index][None, :] > 0)
        right_blocks = right_blocks * matches[:, :, None, None].astype(right_side.dtype)
        return jnp.einsum("gxy,gcyz->cxz", left_blocks.astype(jnp.float32), right_blocks.astype(jnp.float32))

    return lax.map(one_row, jnp.arange(NB, dtype=jnp.int32))


def reference(block_values, block_columns, block_live):
    masked = block_values * block_live[:, :, None, None].astype(jnp.bfloat16)
    squared = filtered_product(masked, masked, block_columns, block_live).astype(jnp.bfloat16)
    cube_part = filtered_product(masked, squared, block_columns, block_live)
    return (1.5 * masked.astype(jnp.float32) - 0.5 * cube_part).astype(jnp.bfloat16)
```

```python
import functools

import jax
import jax.numpy as jnp
from jax import lax
from jax.experimental import pallas as pl
from jax.experimental.pallas import tpu as pltpu
from jax.sharding import PartitionSpec as P

MESH = pl.DeviceIdType.MESH
BS = 256
ROWS = 4
HEAD = 16
NR = 8
NC = 16


class Streams:
    def __init__(self, send_sem, recv_sem):
        self.send_sem, self.recv_sem = send_sem, recv_sem
        self.number = {}
        self.started = []

    def copy(self, key, src, dst, device):
        at = self.number.setdefault(key, len(self.number))
        return pltpu.make_async_remote_copy(
            src_ref=src,
            dst_ref=dst,
            send_sem=self.send_sem.at[at],
            recv_sem=self.recv_sem.at[at],
            device_id=device,
            device_id_type=MESH,
        )

    def send(self, key, src, dst, device):
        copy = self.copy(key, src, dst, device)
        copy.start()
        self.started.append(copy)

    def arrived(self, key, dst, device):
        self.copy(key, dst, dst, device).wait_recv()


def kernel(
    values, columns, live, out, left, right, squared, ext, total, cube, send_sem, recv_sem
):
    row, col = lax.axis_index("row"), lax.axis_index("col")
    y_lo, z = row // 4, row % 4
    y_hi, x, core = col // 8, (col // 2) % 4, col % 2

    def row_of(dy, dz):
        return ((y_lo + dy) % 2) * 4 + (z + dz + 4) % 4

    def col_of(dy, dx, dc):
        return (((y_hi + dy) % 2) * 4 + (x + dx + 4) % 4) * 2 + (core + dc) % 2

    near = {
        "y": (row_of(1, 0), col),
        "z+": (row_of(0, 1), col),
        "z-": (row_of(0, -1), col),
        "x+": (row, col_of(0, 1, 0)),
        "x-": (row, col_of(0, -1, 0)),
        "h": (row, col_of(1, 0, 0)),
        "c": (row, col_of(0, 0, 1)),
    }
    barrier = pltpu.get_barrier_semaphore()
    for device in near.values():
        pl.semaphore_signal(barrier, inc=1, device_id=device, device_id_type=MESH)

    heads = [
        jnp.broadcast_to(columns[j, 0].astype(jnp.float32), (1, BS)) for j in range(ROWS)
    ]
    head = jnp.concatenate(
        heads + [jnp.zeros((HEAD - ROWS, BS), jnp.float32)], axis=0
    ).astype(jnp.bfloat16)
    left[col, 0:HEAD, :] = head
    right[row, 0:HEAD, :] = head
    for j in range(ROWS):
        block = (values[j, 0].astype(jnp.float32) * live[j, 0].astype(jnp.float32)).astype(
            jnp.bfloat16
        )
        left[col, HEAD + j * BS : HEAD + (j + 1) * BS, :] = block
        right[row, HEAD + j * BS : HEAD + (j + 1) * BS, :] = block
    pl.semaphore_wait(barrier, len(near))

    streams = Streams(send_sem, recv_sem)

    def piece(buffer, unit, j):
        if buffer is squared:
            return buffer.at[unit, pl.ds(j * BS, BS)]
        if j == 0:
            return buffer.at[unit, pl.ds(0, HEAD + BS)]
        return buffer.at[unit, pl.ds(HEAD + j * BS, BS)]

    def send(name, buffer, unit, j, way):
        ref = piece(buffer, unit, j)
        streams.send((name, j, way), ref, ref, near[way])

    def arrived(name, buffer, unit, j, way):
        streams.arrived((name, j, way), piece(buffer, unit, j), near[way])

    def right_own(tag, buffer, j):
        for way in ("y", "z+", "z-"):
            send(tag + "own", buffer, row, j, way)

    def right_ring(tag, buffer, j):
        arrived(tag + "own", buffer, row_of(0, -1), j, "z+")
        if j % 2 == 0:
            send(tag + "two", buffer, row_of(0, -1), j, "z+")
        arrived(tag + "own", buffer, row_of(0, 1), j, "z-")
        if j % 2 == 1:
            send(tag + "two", buffer, row_of(0, 1), j, "z-")

    def right_side(tag, buffer, j):
        arrived(tag + "own", buffer, row_of(1, 0), j, "y")
        send(tag + "side", buffer, row_of(1, 0), j, "z+")
        send(tag + "side", buffer, row_of(1, 0), j, "z-")

    def right_two(tag, buffer, j):
        arrived(tag + "two", buffer, row_of(0, 2), j, "z+" if j % 2 == 0 else "z-")
        send(tag + "far", buffer, row_of(0, 2), j, "y")

    def right_end(tag, buffer, j):
        arrived(tag + "side", buffer, row_of(1, -1), j, "z+")
        arrived(tag + "side", buffer, row_of(1, 1), j, "z-")
        arrived(tag + "far", buffer, row_of(1, 2), j, "y")

    def left_own(j):
        for way in ("h", "x+", "x-", "c"):
            send("Lown", left, col, j, way)

    def left_ring(j):
        arrived("Lown", left, col_of(0, -1, 0), j, "x+")
        if j % 2 == 0:
            send("Ltwo", left, col_of(0, -1, 0), j, "x+")
        send("Lm", left, col_of(0, -1, 0), j, "c")
        arrived("Lown", left, col_of(0, 1, 0), j, "x-")
        if j % 2 == 1:
            send("Ltwo", left, col_of(0, 1, 0), j, "x-")
        send("Lp", left, col_of(0, 1, 0), j, "c")

    def left_side(j):
        arrived("Lown", left, col_of(1, 0, 0), j, "h")
        for way in ("x+", "x-", "c"):
            send("Lside", left, col_of(1, 0, 0), j, way)

    def left_side_ring(j):
        arrived("Lside", left, col_of(1, -1, 0), j, "x+")
        if j % 2 == 1:
            send("Lfar", left, col_of(1, -1, 0), j, "x+")
        send("Lsm", left, col_of(1, -1, 0), j, "c")
        arrived("Lside", left, col_of(1, 1, 0), j, "x-")
        if j % 2 == 0:
            send("Lfar", left, col_of(1, 1, 0), j, "x-")
        send("Lsp", left, col_of(1, 1, 0), j, "c")

    def left_two(j):
        arrived("Ltwo", left, col_of(0, 2, 0), j, "x+" if j % 2 == 0 else "x-")
        send("Ltwo", left, col_of(0, 2, 0), j, "c")

    def left_far(j):
        arrived("Lfar", left, col_of(1, 2, 0), j, "x+" if j % 2 == 1 else "x-")
        send("Lfar", left, col_of(1, 2, 0), j, "c")

    def left_end(j):
        arrived("Lown", left, col_of(0, 0, 1), j, "c")
        arrived("Lm", left, col_of(0, -1, 1), j, "c")
        arrived("Lp", left, col_of(0, 1, 1), j, "c")
        arrived("Lside", left, col_of(1, 0, 1), j, "c")
        arrived("Lsm", left, col_of(1, -1, 1), j, "c")
        arrived("Lsp", left, col_of(1, 1, 1), j, "c")
        arrived("Ltwo", left, col_of(0, 2, 1), j, "c")
        arrived("Lfar", left, col_of(1, 2, 1), j, "c")

    def build_ext(i):
        mine = columns[i, 0].astype(jnp.float32)
        alive = (live[i, 0] > 0).astype(jnp.float32)

        def step(r, carry):
            right_head = right[r, 0:HEAD, :].astype(jnp.float32)
            for part in range(2):
                g = 2 * r + part
                own = left[g, 0:HEAD, :].astype(jnp.float32)[i : i + 1]
                block = left[g, HEAD + i * BS : HEAD + (i + 1) * BS, :]
                for b in range(2):
                    j = 2 * part + b
                    met = right_head[j : j + 1]
                    weight = jnp.where((own == float(b)) & (met == mine), alive, 0.0)
                    ext[r, i * BS : (i + 1) * BS, j * BS : (j + 1) * BS] = (
                        block * weight.astype(jnp.bfloat16)
                    )
            return carry

        lax.fori_loop(0, NR, step, 0)

    def square(i):
        total[...] = jnp.zeros_like(total)

        def step(r, carry):
            total[...] += jnp.dot(
                ext[r, i * BS : (i + 1) * BS, :],
                right[r, HEAD:, :],
                preferred_element_type=jnp.float32,
            )
            return carry

        lax.fori_loop(0, NR, step, 0)
        squared[row, i * BS : (i + 1) * BS, :] = total[...].astype(jnp.bfloat16)

    def cube_step(j):
        def step(r, carry):
            cube[...] += jnp.dot(
                ext[r, :, j * BS : (j + 1) * BS],
                squared[r, j * BS : (j + 1) * BS, :],
                preferred_element_type=jnp.float32,
            )
            return carry

        lax.fori_loop(0, NR, step, 0)

    every = range(ROWS)
    for j in every:
        right_own("R", right, j)
        left_own(j)
    cube[...] = jnp.zeros_like(cube)
    for j in every:
        right_ring("R", right, j)
        left_ring(j)
        right_side("R", right, j)
        left_side(j)
    for j in every:
        left_side_ring(j)
        left_two(j)
        right_two("R", right, j)
    for j in every:
        left_far(j)
    for j in every:
        right_end("R", right, j)
    for j in every:
        left_end(j)
        build_ext(j)
        square(j)
        right_own("S", squared, j)
        if j > 0:
            right_ring("S", squared, j - 1)
            right_side("S", squared, j - 1)
    right_ring("S", squared, 3)
    right_side("S", squared, 3)
    for j in every:
        right_two("S", squared, j)
    for j in every:
        right_end("S", squared, j)
        cube_step(j)
    for j in every:
        masked = left[col, HEAD + j * BS : HEAD + (j + 1) * BS, :].astype(jnp.float32)
        out[j, 0] = (1.5 * masked - 0.5 * cube[j * BS : (j + 1) * BS, :]).astype(jnp.bfloat16)
    for copy in streams.started:
        copy.wait_send()


COPIES = ROWS * (15 + 7 + 7)


def body(block_values, block_columns, block_live):
    return pl.pallas_call(
        kernel,
        name="sign_step",
        out_shape=jax.ShapeDtypeStruct(block_values.shape, jnp.bfloat16),
        in_specs=[
            pl.BlockSpec(memory_space=pltpu.VMEM),
            pl.BlockSpec(memory_space=pltpu.SMEM),
            pl.BlockSpec(memory_space=pltpu.SMEM),
        ],
        out_specs=pl.BlockSpec(memory_space=pltpu.VMEM),
        scratch_shapes=[
            pltpu.VMEM((NC, HEAD + ROWS * BS, BS), jnp.bfloat16),
            pltpu.VMEM((NR, HEAD + ROWS * BS, BS), jnp.bfloat16),
            pltpu.VMEM((NR, ROWS * BS, BS), jnp.bfloat16),
            pltpu.VMEM((NR, ROWS * BS, ROWS * BS), jnp.bfloat16),
            pltpu.VMEM((BS, BS), jnp.float32),
            pltpu.VMEM((ROWS * BS, BS), jnp.float32),
            pltpu.SemaphoreType.DMA((COPIES,)),
            pltpu.SemaphoreType.DMA((COPIES,)),
        ],
        compiler_params=pltpu.CompilerParams(
            collective_id=0, has_side_effects=True, vmem_limit_bytes=56 * 1024 * 1024
        ),
    )(block_values, block_columns, block_live)


def solution(mesh):
    return jax.shard_map(
        body,
        mesh=mesh,
        in_specs=(P("row", "col", None, None), P("row", "col"), P("row", "col")),
        out_specs=P("row", "col", None, None),
        check_vma=False,
    )
```

```python
import functools

import jax
import jax.numpy as jnp
from jax import lax
from jax.experimental import pallas as pl
from jax.experimental.pallas import tpu as pltpu
from jax.sharding import PartitionSpec as P

MESH = pl.DeviceIdType.MESH
BS = 256
ROWS = 4
HEAD = 16
NR = 8
NC = 16


class Streams:
    def __init__(self, send_sem, recv_sem):
        self.send_sem, self.recv_sem = send_sem, recv_sem
        self.number = {}
        self.started = []

    def copy(self, key, src, dst, device):
        at = self.number.setdefault(key, len(self.number))
        return pltpu.make_async_remote_copy(
            src_ref=src,
            dst_ref=dst,
            send_sem=self.send_sem.at[at],
            recv_sem=self.recv_sem.at[at],
            device_id=device,
            device_id_type=MESH,
        )

    def send(self, key, src, dst, device):
        copy = self.copy(key, src, dst, device)
        copy.start()
        self.started.append(copy)

    def arrived(self, key, dst, device):
        self.copy(key, dst, dst, device).wait_recv()


def kernel(
    values, columns, live, out, left, right, squared, chosen, cube, send_sem, recv_sem
):
    row, col = lax.axis_index("row"), lax.axis_index("col")
    y_lo, z = row // 4, row % 4
    y_hi, x, core = col // 8, (col // 2) % 4, col % 2

    def row_of(dy, dz):
        return ((y_lo + dy) % 2) * 4 + (z + dz + 4) % 4

    def col_of(dy, dx, dc):
        return (((y_hi + dy) % 2) * 4 + (x + dx + 4) % 4) * 2 + (core + dc) % 2

    near = {
        "y": (row_of(1, 0), col),
        "z+": (row_of(0, 1), col),
        "z-": (row_of(0, -1), col),
        "x+": (row, col_of(0, 1, 0)),
        "x-": (row, col_of(0, -1, 0)),
        "h": (row, col_of(1, 0, 0)),
        "c": (row, col_of(0, 0, 1)),
    }
    barrier = pltpu.get_barrier_semaphore()
    for device in near.values():
        pl.semaphore_signal(barrier, inc=1, device_id=device, device_id_type=MESH)

    heads = [
        jnp.broadcast_to(columns[0, j].astype(jnp.float32), (1, BS)) for j in range(ROWS)
    ]
    head = jnp.concatenate(
        heads + [jnp.zeros((HEAD - ROWS, BS), jnp.float32)], axis=0
    ).astype(jnp.bfloat16)
    left[col, 0:HEAD, :] = head
    right[row, 0:HEAD, :] = head
    for j in range(ROWS):
        block = (values[j, 0].astype(jnp.float32) * live[0, j].astype(jnp.float32)).astype(
            jnp.bfloat16
        )
        left[col, HEAD + j * BS : HEAD + (j + 1) * BS, :] = block
        right[row, HEAD + j * BS : HEAD + (j + 1) * BS, :] = block
    pl.semaphore_wait(barrier, len(near))

    streams = Streams(send_sem, recv_sem)

    def piece(buffer, unit, j):
        if buffer is squared:
            return buffer.at[unit, pl.ds(j * BS, BS)]
        if j == 0:
            return buffer.at[unit, pl.ds(0, HEAD + BS)]
        return buffer.at[unit, pl.ds(HEAD + j * BS, BS)]

    def send(name, buffer, unit, j, way):
        ref = piece(buffer, unit, j)
        streams.send((name, j, way), ref, ref, near[way])

    def arrived(name, buffer, unit, j, way):
        streams.arrived((name, j, way), piece(buffer, unit, j), near[way])

    def right_own(tag, buffer, j):
        for way in ("y", "z+", "z-"):
            send(tag + "own", buffer, row, j, way)

    def right_ring(tag, buffer, j):
        arrived(tag + "own", buffer, row_of(0, -1), j, "z+")
        if j % 2 == 0:
            send(tag + "two", buffer, row_of(0, -1), j, "z+")
        arrived(tag + "own", buffer, row_of(0, 1), j, "z-")
        if j % 2 == 1:
            send(tag + "two", buffer, row_of(0, 1), j, "z-")

    def right_side(tag, buffer, j):
        arrived(tag + "own", buffer, row_of(1, 0), j, "y")
        send(tag + "side", buffer, row_of(1, 0), j, "z+")
        send(tag + "side", buffer, row_of(1, 0), j, "z-")

    def right_two(tag, buffer, j):
        arrived(tag + "two", buffer, row_of(0, 2), j, "z+" if j % 2 == 0 else "z-")
        send(tag + "far", buffer, row_of(0, 2), j, "y")

    def right_end(tag, buffer, j):
        arrived(tag + "side", buffer, row_of(1, -1), j, "z+")
        arrived(tag + "side", buffer, row_of(1, 1), j, "z-")
        arrived(tag + "far", buffer, row_of(1, 2), j, "y")

    def left_own(j):
        for way in ("x+", "x-", "c"):
            send("Lown", left, col, j, way)

    def left_hop(j):
        send("Lown", left, col, j, "h")

    def left_ring(j):
        arrived("Lown", left, col_of(0, -1, 0), j, "x+")
        if j % 2 == 0:
            send("Ltwo", left, col_of(0, -1, 0), j, "x+")
        send("Lm", left, col_of(0, -1, 0), j, "c")
        arrived("Lown", left, col_of(0, 1, 0), j, "x-")
        if j % 2 == 1:
            send("Ltwo", left, col_of(0, 1, 0), j, "x-")
        send("Lp", left, col_of(0, 1, 0), j, "c")

    def left_side(j):
        arrived("Lown", left, col_of(1, 0, 0), j, "h")
        for way in ("x+", "x-", "c"):
            send("Lside", left, col_of(1, 0, 0), j, way)

    def left_side_ring(j):
        arrived("Lside", left, col_of(1, -1, 0), j, "x+")
        if j % 2 == 1:
            send("Lfar", left, col_of(1, -1, 0), j, "x+")
        send("Lsm", left, col_of(1, -1, 0), j, "c")
        arrived("Lside", left, col_of(1, 1, 0), j, "x-")
        if j % 2 == 0:
            send("Lfar", left, col_of(1, 1, 0), j, "x-")
        send("Lsp", left, col_of(1, 1, 0), j, "c")

    def left_two(j):
        arrived("Ltwo", left, col_of(0, 2, 0), j, "x+" if j % 2 == 0 else "x-")
        send("Ltwo", left, col_of(0, 2, 0), j, "c")

    def left_far(j):
        arrived("Lfar", left, col_of(1, 2, 0), j, "x+" if j % 2 == 1 else "x-")
        send("Lfar", left, col_of(1, 2, 0), j, "c")

    def left_end(j):
        arrived("Lown", left, col_of(0, 0, 1), j, "c")
        arrived("Lm", left, col_of(0, -1, 1), j, "c")
        arrived("Lp", left, col_of(0, 1, 1), j, "c")
        arrived("Lside", left, col_of(1, 0, 1), j, "c")
        arrived("Lsm", left, col_of(1, -1, 1), j, "c")
        arrived("Lsp", left, col_of(1, 1, 1), j, "c")
        arrived("Ltwo", left, col_of(0, 2, 1), j, "c")
        arrived("Lfar", left, col_of(1, 2, 1), j, "c")

    def select(buffer, first, i, parts):
        mine = columns[0, i].astype(jnp.float32)
        alive = (live[0, i] > 0).astype(jnp.float32)
        for r in range(NR):
            right_head = right[r, 0:HEAD, :].astype(jnp.float32)
            for part in parts:
                g = 2 * r + part
                own = left[g, 0:HEAD, :].astype(jnp.float32)[i : i + 1]
                weights = []
                for b in range(2):
                    met = right_head[2 * part + b : 2 * part + b + 1]
                    weights.append(
                        jnp.where((own == float(b)) & (met == mine), alive, 0.0).astype(
                            jnp.bfloat16
                        )
                    )
                at = first + 2 * part * BS
                chosen[g * BS : (g + 1) * BS, :] = (
                    buffer[r, at : at + BS, :] * weights[0]
                    + buffer[r, at + BS : at + 2 * BS, :] * weights[1]
                )

    def product(i, parts):
        groups = [2 * r + part for r in range(NR) for part in parts]
        rows = jnp.concatenate(
            [left[g, HEAD + i * BS : HEAD + (i + 1) * BS, :] for g in groups], axis=1
        )
        return jnp.dot(
            rows,
            jnp.concatenate([chosen[g * BS : (g + 1) * BS, :] for g in groups], axis=0),
            preferred_element_type=jnp.float32,
        )

    def square(i):
        select(right, HEAD, i, (0, 1))
        squared[row, i * BS : (i + 1) * BS, :] = product(i, (0, 1)).astype(jnp.bfloat16)

    def cube_even():
        for i in range(ROWS):
            select(squared, 0, i, (0,))
            cube[i * BS : (i + 1) * BS, :] = product(i, (0,))

    def finish():
        for i in range(ROWS):
            select(squared, 0, i, (1,))
            cube_part = cube[i * BS : (i + 1) * BS, :] + product(i, (1,))
            masked = left[col, HEAD + i * BS : HEAD + (i + 1) * BS, :].astype(jnp.float32)
            out[i, 0] = (1.5 * masked - 0.5 * cube_part).astype(jnp.bfloat16)

    every = range(ROWS)
    for j in every:
        right_own("R", right, j)
        left_own(j)
        left_hop(j)
    for j in every:
        right_ring("R", right, j)
        left_ring(j)
        right_side("R", right, j)
        left_side(j)
    for j in every:
        left_side_ring(j)
        left_two(j)
        right_two("R", right, j)
    for j in every:
        left_far(j)
    for j in every:
        right_end("R", right, j)
    for j in every:
        left_end(j)
        square(j)
        right_own("S", squared, j)
        if j > 0:
            right_ring("S", squared, j - 1)
            right_side("S", squared, j - 1)
    right_ring("S", squared, 3)
    right_side("S", squared, 3)
    for j in every:
        right_two("S", squared, j)
    for j in (0, 1):
        right_end("S", squared, j)
    cube_even()
    for j in (2, 3):
        right_end("S", squared, j)
    finish()
    for copy in streams.started:
        copy.wait_send()


COPIES = ROWS * (15 + 7 + 7)


def body(block_values, block_columns, block_live):
    return pl.pallas_call(
        kernel,
        name="sign_step",
        out_shape=jax.ShapeDtypeStruct(block_values.shape, jnp.bfloat16),
        in_specs=[
            pl.BlockSpec(memory_space=pltpu.VMEM),
            pl.BlockSpec(memory_space=pltpu.SMEM),
            pl.BlockSpec(memory_space=pltpu.SMEM),
        ],
        out_specs=pl.BlockSpec(memory_space=pltpu.VMEM),
        scratch_shapes=[
            pltpu.VMEM((NC, HEAD + ROWS * BS, BS), jnp.bfloat16),
            pltpu.VMEM((NR, HEAD + ROWS * BS, BS), jnp.bfloat16),
            pltpu.VMEM((NR, ROWS * BS, BS), jnp.bfloat16),
            pltpu.VMEM((NC * BS, BS), jnp.bfloat16),
            pltpu.VMEM((ROWS * BS, BS), jnp.float32),
            pltpu.SemaphoreType.DMA((COPIES,)),
            pltpu.SemaphoreType.DMA((COPIES,)),
        ],
        compiler_params=pltpu.CompilerParams(
            collective_id=0, has_side_effects=True, vmem_limit_bytes=56 * 1024 * 1024
        ),
    )(block_values, block_columns.T, block_live.T)


def solution(mesh):
    return jax.shard_map(
        body,
        mesh=mesh,
        in_specs=(P("row", "col", None, None), P("row", "col"), P("row", "col")),
        out_specs=P("row", "col", None, None),
        check_vma=False,
    )
```

```python
import functools

import jax
import jax.numpy as jnp
from jax import lax
from jax.experimental import pallas as pl
from jax.experimental.pallas import tpu as pltpu
from jax.sharding import PartitionSpec as P

MESH = pl.DeviceIdType.MESH
BS = 256
ROWS = 4
HEAD = 16
NR = 8
NC = 16


PATHS = {
    ("R", "two"): "++--",
    ("R", "far"): "++yy",
    ("R", "m"): "zzzy",
    ("R", "p"): "zzzz",
    ("S", "two"): "--++",
    ("S", "far"): "y-y+",
    ("S", "m"): "yzyz",
    ("S", "p"): "yzyz",
    ("L", "two"): "-+-+",
    ("L", "far"): "--++",
}

ORDER = (
    ("R", "own", 0),
    ("R", "own", 1),
    ("R", "own", 3),
    ("L", "own", 0),
    ("L", "own", 1),
    ("L", "p", 0),
    ("L", "hop", 1),
    ("L", "own", 3),
    ("L", "hop", 0),
    ("R", "side", 1),
    ("L", "own", 2),
    ("R", "own", 2),
    ("R", "side", 0),
    ("L", "m", 1),
    ("R", "m", 1),
    ("L", "m", 3),
    ("R", "p", 3),
    ("L", "hop", 3),
    ("L", "hop", 2),
    ("L", "p", 3),
    ("L", "side", 1),
    ("R", "p", 0),
    ("R", "m", 3),
    ("L", "m", 0),
    ("R", "p", 1),
    ("R", "m", 0),
    ("R", "p", 2),
    ("L", "side", 0),
    ("L", "sp", 1),
    ("R", "side", 3),
    ("R", "side", 2),
    ("L", "sp", 0),
    ("R", "two", 3),
    ("L", "side", 3),
    ("R", "sideM", 1),
    ("L", "sm", 0),
    ("R", "two", 1),
    ("L", "p", 2),
    ("R", "sideM", 0),
    ("R", "sideP", 1),
    ("R", "two", 2),
    ("L", "two", 3),
    ("L", "side", 2),
    ("L", "two", 1),
    ("L", "p", 1),
    ("L", "far", 1),
    ("R", "two", 0),
    ("R", "sideP", 3),
    ("R", "m", 2),
    ("L", "far", 0),
    ("L", "sm", 3),
    ("L", "sm", 1),
    ("L", "two", 0),
    ("R", "sideM", 3),
    ("L", "sp", 3),
    ("R", "sideM", 2),
    ("L", "end", 0),
    ("R", "sideP", 2),
    ("L", "sm", 2),
    ("R", "far", 3),
    ("R", "far", 1),
    ("L", "end", 1),
    ("L", "m", 2),
    ("R", "sideP", 0),
    ("R", "far", 2),
    ("R", "far", 0),
    ("C", "square", 0),
    ("S", "own", 0),
    ("C", "square", 1),
    ("S", "own", 1),
    ("L", "far", 3),
    ("L", "far", 2),
    ("L", "end", 3),
    ("C", "square", 3),
    ("L", "two", 2),
    ("S", "own", 3),
    ("L", "sp", 2),
    ("S", "m", 0),
    ("S", "p", 0),
    ("L", "end", 2),
    ("C", "square", 2),
    ("S", "m", 1),
    ("S", "own", 2),
    ("S", "side", 1),
    ("S", "side", 3),
    ("S", "m", 2),
    ("S", "p", 1),
    ("S", "p", 2),
    ("S", "sideP", 1),
    ("S", "m", 3),
    ("S", "two", 0),
    ("S", "sideM", 3),
    ("S", "sideP", 3),
    ("S", "two", 2),
    ("S", "far", 1),
    ("S", "sideM", 0),
    ("S", "p", 3),
    ("S", "side", 0),
    ("S", "far", 3),
    ("S", "sideP", 0),
    ("S", "sideP", 2),
    ("S", "two", 3),
    ("S", "far", 0),
    ("S", "sideM", 2),
    ("S", "side", 2),
    ("S", "two", 1),
    ("S", "sideM", 1),
    ("C", "even", 0),
    ("S", "far", 2),
    ("C", "finish", 0),
)


class Streams:
    def __init__(self, send_sem, recv_sem):
        self.send_sem, self.recv_sem = send_sem, recv_sem
        self.number = {}
        self.started = []

    def copy(self, key, src, dst, device):
        at = self.number.setdefault(key, len(self.number))
        return pltpu.make_async_remote_copy(
            src_ref=src,
            dst_ref=dst,
            send_sem=self.send_sem.at[at],
            recv_sem=self.recv_sem.at[at],
            device_id=device,
            device_id_type=MESH,
        )

    def send(self, key, src, dst, device):
        copy = self.copy(key, src, dst, device)
        copy.start()
        self.started.append(copy)

    def arrived(self, key, dst, device):
        self.copy(key, dst, dst, device).wait_recv()


def kernel(
    values, columns, live, out, left, right, squared, chosen, cube, send_sem, recv_sem
):
    row, col = lax.axis_index("row"), lax.axis_index("col")
    y_lo, z = row // 4, row % 4
    y_hi, x, core = col // 8, (col // 2) % 4, col % 2

    def row_of(dy, dz):
        return ((y_lo + dy) % 2) * 4 + (z + dz + 4) % 4

    def col_of(dy, dx, dc):
        return (((y_hi + dy) % 2) * 4 + (x + dx + 4) % 4) * 2 + (core + dc) % 2

    near = {
        "y": (row_of(1, 0), col),
        "z+": (row_of(0, 1), col),
        "z-": (row_of(0, -1), col),
        "x+": (row, col_of(0, 1, 0)),
        "x-": (row, col_of(0, -1, 0)),
        "h": (row, col_of(1, 0, 0)),
        "c": (row, col_of(0, 0, 1)),
    }
    barrier = pltpu.get_barrier_semaphore()
    for device in near.values():
        pl.semaphore_signal(barrier, inc=1, device_id=device, device_id_type=MESH)

    heads = [
        jnp.broadcast_to(columns[0, j].astype(jnp.float32), (1, BS)) for j in range(ROWS)
    ]
    head = jnp.concatenate(
        heads + [jnp.zeros((HEAD - ROWS, BS), jnp.float32)], axis=0
    ).astype(jnp.bfloat16)
    left[col, 0:HEAD, :] = head
    right[row, 0:HEAD, :] = head
    for j in range(ROWS):
        block = (values[j, 0].astype(jnp.float32) * live[0, j].astype(jnp.float32)).astype(
            jnp.bfloat16
        )
        left[col, HEAD + j * BS : HEAD + (j + 1) * BS, :] = block
        right[row, HEAD + j * BS : HEAD + (j + 1) * BS, :] = block
    pl.semaphore_wait(barrier, len(near))

    streams = Streams(send_sem, recv_sem)

    def piece(buffer, unit, j):
        if buffer is squared:
            return buffer.at[unit, pl.ds(j * BS, BS)]
        if j == 0:
            return buffer.at[unit, pl.ds(0, HEAD + BS)]
        return buffer.at[unit, pl.ds(HEAD + j * BS, BS)]

    def send(name, buffer, unit, j, way):
        ref = piece(buffer, unit, j)
        streams.send((name, j, way), ref, ref, near[way])

    def arrived(name, buffer, unit, j, way):
        streams.arrived((name, j, way), piece(buffer, unit, j), near[way])

    def right_step(tag, buffer, name, j):
        two, far, side_m, side_p = (PATHS[tag, k][j] for k in ("two", "far", "m", "p"))
        if name == "own":
            for way in ("y", "z+", "z-"):
                send(tag + "own", buffer, row, j, way)
        elif name == "m":
            arrived(tag + "own", buffer, row_of(0, -1), j, "z+")
            if two == "+":
                send(tag + "two", buffer, row_of(0, -1), j, "z+")
            if side_m == "y":
                send(tag + "sideM", buffer, row_of(0, -1), j, "y")
        elif name == "p":
            arrived(tag + "own", buffer, row_of(0, 1), j, "z-")
            if two == "-":
                send(tag + "two", buffer, row_of(0, 1), j, "z-")
            if side_p == "y":
                send(tag + "sideP", buffer, row_of(0, 1), j, "y")
        elif name == "side":
            arrived(tag + "own", buffer, row_of(1, 0), j, "y")
            if side_m == "z":
                send(tag + "sideM", buffer, row_of(1, 0), j, "z+")
            if side_p == "z":
                send(tag + "sideP", buffer, row_of(1, 0), j, "z-")
        elif name == "two":
            arrived(tag + "two", buffer, row_of(0, 2), j, "z" + two)
            if far == "y":
                send(tag + "far", buffer, row_of(0, 2), j, "y")
        elif name == "sideM":
            arrived(tag + "sideM", buffer, row_of(1, -1), j, "z+" if side_m == "z" else "y")
            if far == "+":
                send(tag + "far", buffer, row_of(1, -1), j, "z+")
        elif name == "sideP":
            arrived(tag + "sideP", buffer, row_of(1, 1), j, "z-" if side_p == "z" else "y")
            if far == "-":
                send(tag + "far", buffer, row_of(1, 1), j, "z-")
        elif name == "far":
            arrived(tag + "far", buffer, row_of(1, 2), j, "y" if far == "y" else "z" + far)

    def left_step(name, j):
        two, far = (PATHS["L", k][j] for k in ("two", "far"))
        if name == "own":
            for way in ("x+", "x-", "c"):
                send("Lown", left, col, j, way)
        elif name == "hop":
            send("Lown", left, col, j, "h")
        elif name == "m":
            arrived("Lown", left, col_of(0, -1, 0), j, "x+")
            if two == "+":
                send("Ltwo", left, col_of(0, -1, 0), j, "x+")
            send("Lm", left, col_of(0, -1, 0), j, "c")
        elif name == "p":
            arrived("Lown", left, col_of(0, 1, 0), j, "x-")
            if two == "-":
                send("Ltwo", left, col_of(0, 1, 0), j, "x-")
            send("Lp", left, col_of(0, 1, 0), j, "c")
        elif name == "side":
            arrived("Lown", left, col_of(1, 0, 0), j, "h")
            for way in ("x+", "x-", "c"):
                send("Lside", left, col_of(1, 0, 0), j, way)
        elif name == "sm":
            arrived("Lside", left, col_of(1, -1, 0), j, "x+")
            if far == "+":
                send("Lfar", left, col_of(1, -1, 0), j, "x+")
            send("Lsm", left, col_of(1, -1, 0), j, "c")
        elif name == "sp":
            arrived("Lside", left, col_of(1, 1, 0), j, "x-")
            if far == "-":
                send("Lfar", left, col_of(1, 1, 0), j, "x-")
            send("Lsp", left, col_of(1, 1, 0), j, "c")
        elif name == "two":
            arrived("Ltwo", left, col_of(0, 2, 0), j, "x" + two)
            send("Ltwo", left, col_of(0, 2, 0), j, "c")
        elif name == "far":
            arrived("Lfar", left, col_of(1, 2, 0), j, "x" + far)
            send("Lfar", left, col_of(1, 2, 0), j, "c")
        elif name == "end":
            arrived("Lown", left, col_of(0, 0, 1), j, "c")
            arrived("Lm", left, col_of(0, -1, 1), j, "c")
            arrived("Lp", left, col_of(0, 1, 1), j, "c")
            arrived("Lside", left, col_of(1, 0, 1), j, "c")
            arrived("Lsm", left, col_of(1, -1, 1), j, "c")
            arrived("Lsp", left, col_of(1, 1, 1), j, "c")
            arrived("Ltwo", left, col_of(0, 2, 1), j, "c")
            arrived("Lfar", left, col_of(1, 2, 1), j, "c")

    def select(buffer, first, i, parts):
        mine = columns[0, i].astype(jnp.float32)
        alive = (live[0, i] > 0).astype(jnp.float32)
        for r in range(NR):
            right_head = right[r, 0:HEAD, :].astype(jnp.float32)
            for part in parts:
                g = 2 * r + part
                own = left[g, 0:HEAD, :].astype(jnp.float32)[i : i + 1]
                weights = []
                for b in range(2):
                    met = right_head[2 * part + b : 2 * part + b + 1]
                    weights.append(
                        jnp.where((own == float(b)) & (met == mine), alive, 0.0).astype(
                            jnp.bfloat16
                        )
                    )
                at = first + 2 * part * BS
                chosen[g * BS : (g + 1) * BS, :] = (
                    buffer[r, at : at + BS, :] * weights[0]
                    + buffer[r, at + BS : at + 2 * BS, :] * weights[1]
                )

    def product(i, parts):
        groups = [2 * r + part for r in range(NR) for part in parts]
        rows = jnp.concatenate(
            [left[g, HEAD + i * BS : HEAD + (i + 1) * BS, :] for g in groups], axis=1
        )
        return jnp.dot(
            rows,
            jnp.concatenate([chosen[g * BS : (g + 1) * BS, :] for g in groups], axis=0),
            preferred_element_type=jnp.float32,
        )

    def square(i):
        select(right, HEAD, i, (0, 1))
        squared[row, i * BS : (i + 1) * BS, :] = product(i, (0, 1)).astype(jnp.bfloat16)

    def cube_even():
        for i in range(ROWS):
            select(squared, 0, i, (0,))
            cube[i * BS : (i + 1) * BS, :] = product(i, (0,))

    def finish():
        for i in range(ROWS):
            select(squared, 0, i, (1,))
            cube_part = cube[i * BS : (i + 1) * BS, :] + product(i, (1,))
            masked = left[col, HEAD + i * BS : HEAD + (i + 1) * BS, :].astype(jnp.float32)
            out[i, 0] = (1.5 * masked - 0.5 * cube_part).astype(jnp.bfloat16)

    for tag, name, j in ORDER:
        if tag == "R":
            right_step(tag, right, name, j)
        elif tag == "S":
            right_step(tag, squared, name, j)
        elif tag == "L":
            left_step(name, j)
        elif name == "square":
            square(j)
        elif name == "even":
            cube_even()
        else:
            finish()
    for copy in streams.started:
        copy.wait_send()


COPIES = ROWS * (15 + 7 + 7)


def body(block_values, block_columns, block_live):
    return pl.pallas_call(
        kernel,
        name="sign_step",
        out_shape=jax.ShapeDtypeStruct(block_values.shape, jnp.bfloat16),
        in_specs=[
            pl.BlockSpec(memory_space=pltpu.VMEM),
            pl.BlockSpec(memory_space=pltpu.SMEM),
            pl.BlockSpec(memory_space=pltpu.SMEM),
        ],
        out_specs=pl.BlockSpec(memory_space=pltpu.VMEM),
        scratch_shapes=[
            pltpu.VMEM((NC, HEAD + ROWS * BS, BS), jnp.bfloat16),
            pltpu.VMEM((NR, HEAD + ROWS * BS, BS), jnp.bfloat16),
            pltpu.VMEM((NR, ROWS * BS, BS), jnp.bfloat16),
            pltpu.VMEM((NC * BS, BS), jnp.bfloat16),
            pltpu.VMEM((ROWS * BS, BS), jnp.float32),
            pltpu.SemaphoreType.DMA((COPIES,)),
            pltpu.SemaphoreType.DMA((COPIES,)),
        ],
        compiler_params=pltpu.CompilerParams(
            collective_id=0, has_side_effects=True, vmem_limit_bytes=56 * 1024 * 1024
        ),
    )(block_values, block_columns.T, block_live.T)


def solution(mesh):
    return jax.shard_map(
        body,
        mesh=mesh,
        in_specs=(P("row", "col", None, None), P("row", "col"), P("row", "col")),
        out_specs=P("row", "col", None, None),
        check_vma=False,
    )
```

```python
import functools

import jax
import jax.numpy as jnp
from jax import lax
from jax.experimental import pallas as pl
from jax.experimental.pallas import tpu as pltpu
from jax.sharding import PartitionSpec as P

MESH = pl.DeviceIdType.MESH
BS = 256
ROWS = 4
HEAD = 16
PIECES = 4
PIECE = ROWS * BS // PIECES
NR = 8
NC = 16


PATHS = {
    ("R", "two"): "--++",
    ("R", "far"): "+-y-",
    ("R", "m"): "zzzz",
    ("R", "p"): "yzyz",
    ("S", "two"): "-+-+",
    ("S", "far"): "y+y-",
    ("S", "m"): "zyzz",
    ("S", "p"): "yzzy",
    ("L", "two"): "-+-+",
    ("L", "far"): "+-+-",
}

ORDER = (
    ("R", "own", 3),
    ("R", "own", 1),
    ("L", "hop", 1),
    ("L", "hop", 0),
    ("R", "own", 0),
    ("L", "own", 3),
    ("R", "own", 2),
    ("L", "own", 0),
    ("L", "own", 2),
    ("L", "hop", 3),
    ("R", "side", 1),
    ("R", "side", 3),
    ("L", "hop", 2),
    ("L", "m", 3),
    ("L", "p", 0),
    ("L", "own", 1),
    ("L", "side", 1),
    ("L", "two", 0),
    ("L", "m", 2),
    ("L", "side", 0),
    ("R", "m", 2),
    ("R", "m", 1),
    ("R", "side", 0),
    ("R", "p", 0),
    ("L", "m", 1),
    ("R", "p", 1),
    ("R", "m", 3),
    ("R", "side", 2),
    ("L", "sp", 1),
    ("R", "sideP", 1),
    ("R", "two", 2),
    ("L", "sm", 0),
    ("R", "sideM", 1),
    ("L", "m", 0),
    ("L", "side", 3),
    ("L", "p", 1),
    ("R", "p", 2),
    ("R", "sideP", 3),
    ("R", "two", 0),
    ("L", "two", 3),
    ("L", "two", 1),
    ("L", "side", 2),
    ("L", "sm", 1),
    ("R", "two", 1),
    ("R", "sideM", 0),
    ("L", "p", 3),
    ("R", "two", 3),
    ("L", "far", 1),
    ("L", "sp", 3),
    ("R", "p", 3),
    ("L", "end", 1),
    ("L", "far", 0),
    ("R", "sideM", 3),
    ("L", "sp", 0),
    ("R", "sideM", 2),
    ("L", "sp", 2),
    ("R", "m", 0),
    ("R", "far", 1),
    ("L", "end", 0),
    ("R", "far", 3),
    ("L", "p", 2),
    ("R", "far", 2),
    ("R", "sideP", 0),
    ("L", "sm", 3),
    ("R", "far", 0),
    ("R", "sideP", 2),
    ("C", "square", 0),
    ("S", "own", 0),
    ("C", "square", 1),
    ("L", "far", 3),
    ("L", "sm", 2),
    ("S", "own", 1),
    ("L", "end", 3),
    ("C", "square", 3),
    ("S", "own", 3),
    ("L", "far", 2),
    ("S", "p", 0),
    ("S", "side", 0),
    ("L", "two", 2),
    ("L", "end", 2),
    ("C", "square", 2),
    ("S", "m", 1),
    ("S", "own", 2),
    ("S", "side", 1),
    ("S", "sideP", 0),
    ("S", "side", 3),
    ("S", "m", 0),
    ("S", "p", 2),
    ("S", "p", 3),
    ("S", "two", 0),
    ("S", "sideM", 1),
    ("S", "side", 2),
    ("S", "two", 2),
    ("S", "m", 3),
    ("S", "sideP", 3),
    ("S", "far", 1),
    ("S", "p", 1),
    ("S", "m", 2),
    ("S", "two", 1),
    ("S", "sideP", 1),
    ("S", "sideM", 2),
    ("S", "sideM", 0),
    ("S", "sideM", 3),
    ("S", "far", 0),
    ("C", "even", 0),
    ("S", "far", 2),
    ("S", "sideP", 2),
    ("S", "far", 3),
    ("S", "two", 3),
    ("C", "finish", 0),
)


class Streams:
    def __init__(self, send_sem, recv_sem):
        self.send_sem, self.recv_sem = send_sem, recv_sem
        self.number = {}
        self.started = []

    def copy(self, key, src, dst, device):
        at = self.number.setdefault(key, len(self.number))
        return pltpu.make_async_remote_copy(
            src_ref=src,
            dst_ref=dst,
            send_sem=self.send_sem.at[at],
            recv_sem=self.recv_sem.at[at],
            device_id=device,
            device_id_type=MESH,
        )

    def send(self, key, src, dst, device):
        copy = self.copy(key, src, dst, device)
        copy.start()
        self.started.append(copy)

    def arrived(self, key, dst, device):
        self.copy(key, dst, dst, device).wait_recv()


def kernel(
    values_in, columns_in, live_in, out, values, columns, live, left, right, squared, chosen, cube, in_sem, send_sem, recv_sem
):
    row, col = lax.axis_index("row"), lax.axis_index("col")
    y_lo, z = row // 4, row % 4
    y_hi, x, core = col // 8, (col // 2) % 4, col % 2

    def row_of(dy, dz):
        return ((y_lo + dy) % 2) * 4 + (z + dz + 4) % 4

    def col_of(dy, dx, dc):
        return (((y_hi + dy) % 2) * 4 + (x + dx + 4) % 4) * 2 + (core + dc) % 2

    near = {
        "y": (row_of(1, 0), col),
        "z+": (row_of(0, 1), col),
        "z-": (row_of(0, -1), col),
        "x+": (row, col_of(0, 1, 0)),
        "x-": (row, col_of(0, -1, 0)),
        "h": (row, col_of(1, 0, 0)),
        "c": (row, col_of(0, 0, 1)),
    }
    barrier = pltpu.get_barrier_semaphore()
    for device in near.values():
        pl.semaphore_signal(barrier, inc=1, device_id=device, device_id_type=MESH)

    fetches = [
        pltpu.make_async_copy(source, target, in_sem.at[at])
        for at, (source, target) in enumerate(
            ((columns_in, columns), (live_in, live), (values_in, values))
        )
    ]
    for fetch in fetches:
        fetch.start()
    for fetch in fetches:
        fetch.wait()

    heads = [
        jnp.broadcast_to(columns[0, j].astype(jnp.float32), (1, BS)) for j in range(ROWS)
    ]
    head = jnp.concatenate(
        heads + [jnp.zeros((HEAD - ROWS, BS), jnp.float32)], axis=0
    ).astype(jnp.bfloat16)
    left[col, 0:HEAD, :] = head
    right[row, 0:HEAD, :] = head
    for j in range(ROWS):
        block = (values[j, 0].astype(jnp.float32) * live[0, j].astype(jnp.float32)).astype(
            jnp.bfloat16
        )
        left[col, HEAD + j * BS : HEAD + (j + 1) * BS, :] = block
        right[row, HEAD + j * BS : HEAD + (j + 1) * BS, :] = block
    pl.semaphore_wait(barrier, len(near))

    streams = Streams(send_sem, recv_sem)

    def piece(buffer, unit, j):
        if buffer is squared:
            return buffer.at[unit, pl.ds(j * PIECE, PIECE)]
        if j == 0:
            return buffer.at[unit, pl.ds(0, HEAD + PIECE)]
        return buffer.at[unit, pl.ds(HEAD + j * PIECE, PIECE)]

    def send(name, buffer, unit, j, way):
        ref = piece(buffer, unit, j)
        streams.send((name, j, way), ref, ref, near[way])

    def arrived(name, buffer, unit, j, way):
        streams.arrived((name, j, way), piece(buffer, unit, j), near[way])

    def right_step(tag, buffer, name, j):
        two, far, side_m, side_p = (PATHS[tag, k][j] for k in ("two", "far", "m", "p"))
        if name == "own":
            for way in ("y", "z+", "z-"):
                send(tag + "own", buffer, row, j, way)
        elif name == "m":
            arrived(tag + "own", buffer, row_of(0, -1), j, "z+")
            if two == "+":
                send(tag + "two", buffer, row_of(0, -1), j, "z+")
            if side_m == "y":
                send(tag + "sideM", buffer, row_of(0, -1), j, "y")
        elif name == "p":
            arrived(tag + "own", buffer, row_of(0, 1), j, "z-")
            if two == "-":
                send(tag + "two", buffer, row_of(0, 1), j, "z-")
            if side_p == "y":
                send(tag + "sideP", buffer, row_of(0, 1), j, "y")
        elif name == "side":
            arrived(tag + "own", buffer, row_of(1, 0), j, "y")
            if side_m == "z":
                send(tag + "sideM", buffer, row_of(1, 0), j, "z+")
            if side_p == "z":
                send(tag + "sideP", buffer, row_of(1, 0), j, "z-")
        elif name == "two":
            arrived(tag + "two", buffer, row_of(0, 2), j, "z" + two)
            if far == "y":
                send(tag + "far", buffer, row_of(0, 2), j, "y")
        elif name == "sideM":
            arrived(tag + "sideM", buffer, row_of(1, -1), j, "z+" if side_m == "z" else "y")
            if far == "+":
                send(tag + "far", buffer, row_of(1, -1), j, "z+")
        elif name == "sideP":
            arrived(tag + "sideP", buffer, row_of(1, 1), j, "z-" if side_p == "z" else "y")
            if far == "-":
                send(tag + "far", buffer, row_of(1, 1), j, "z-")
        elif name == "far":
            arrived(tag + "far", buffer, row_of(1, 2), j, "y" if far == "y" else "z" + far)

    def left_step(name, j):
        two, far = (PATHS["L", k][j] for k in ("two", "far"))
        if name == "own":
            for way in ("x+", "x-", "c"):
                send("Lown", left, col, j, way)
        elif name == "hop":
            send("Lown", left, col, j, "h")
        elif name == "m":
            arrived("Lown", left, col_of(0, -1, 0), j, "x+")
            if two == "+":
                send("Ltwo", left, col_of(0, -1, 0), j, "x+")
            send("Lm", left, col_of(0, -1, 0), j, "c")
        elif name == "p":
            arrived("Lown", left, col_of(0, 1, 0), j, "x-")
            if two == "-":
                send("Ltwo", left, col_of(0, 1, 0), j, "x-")
            send("Lp", left, col_of(0, 1, 0), j, "c")
        elif name == "side":
            arrived("Lown", left, col_of(1, 0, 0), j, "h")
            for way in ("x+", "x-", "c"):
                send("Lside", left, col_of(1, 0, 0), j, way)
        elif name == "sm":
            arrived("Lside", left, col_of(1, -1, 0), j, "x+")
            if far == "+":
                send("Lfar", left, col_of(1, -1, 0), j, "x+")
            send("Lsm", left, col_of(1, -1, 0), j, "c")
        elif name == "sp":
            arrived("Lside", left, col_of(1, 1, 0), j, "x-")
            if far == "-":
                send("Lfar", left, col_of(1, 1, 0), j, "x-")
            send("Lsp", left, col_of(1, 1, 0), j, "c")
        elif name == "two":
            arrived("Ltwo", left, col_of(0, 2, 0), j, "x" + two)
            send("Ltwo", left, col_of(0, 2, 0), j, "c")
        elif name == "far":
            arrived("Lfar", left, col_of(1, 2, 0), j, "x" + far)
            send("Lfar", left, col_of(1, 2, 0), j, "c")
        elif name == "end":
            arrived("Lown", left, col_of(0, 0, 1), j, "c")
            arrived("Lm", left, col_of(0, -1, 1), j, "c")
            arrived("Lp", left, col_of(0, 1, 1), j, "c")
            arrived("Lside", left, col_of(1, 0, 1), j, "c")
            arrived("Lsm", left, col_of(1, -1, 1), j, "c")
            arrived("Lsp", left, col_of(1, 1, 1), j, "c")
            arrived("Ltwo", left, col_of(0, 2, 1), j, "c")
            arrived("Lfar", left, col_of(1, 2, 1), j, "c")

    def select(buffer, first, i, parts):
        mine = columns[0, i].astype(jnp.float32)
        alive = (live[0, i] > 0).astype(jnp.float32)
        for r in range(NR):
            right_head = right[r, 0:HEAD, :].astype(jnp.float32)
            for part in parts:
                g = 2 * r + part
                own = left[g, 0:HEAD, :].astype(jnp.float32)[i : i + 1]
                weights = []
                for b in range(2):
                    met = right_head[2 * part + b : 2 * part + b + 1]
                    weights.append(
                        jnp.where((own == float(b)) & (met == mine), alive, 0.0).astype(
                            jnp.bfloat16
                        )
                    )
                at = first + 2 * part * BS
                chosen[g * BS : (g + 1) * BS, :] = (
                    buffer[r, at : at + BS, :] * weights[0]
                    + buffer[r, at + BS : at + 2 * BS, :] * weights[1]
                )

    def product(i, parts):
        groups = [2 * r + part for r in range(NR) for part in parts]
        rows = jnp.concatenate(
            [left[g, HEAD + i * BS : HEAD + (i + 1) * BS, :] for g in groups], axis=1
        )
        return jnp.dot(
            rows,
            jnp.concatenate([chosen[g * BS : (g + 1) * BS, :] for g in groups], axis=0),
            preferred_element_type=jnp.float32,
        )

    def square(i):
        select(right, HEAD, i, (0, 1))
        squared[row, i * BS : (i + 1) * BS, :] = product(i, (0, 1)).astype(jnp.bfloat16)

    def cube_even():
        for i in range(ROWS):
            select(squared, 0, i, (0,))
            cube[i * BS : (i + 1) * BS, :] = product(i, (0,))

    def finish():
        for i in range(ROWS):
            select(squared, 0, i, (1,))
            cube_part = cube[i * BS : (i + 1) * BS, :] + product(i, (1,))
            masked = left[col, HEAD + i * BS : HEAD + (i + 1) * BS, :].astype(jnp.float32)
            out[i, 0] = (1.5 * masked - 0.5 * cube_part).astype(jnp.bfloat16)

    for tag, name, j in ORDER:
        if tag == "R":
            right_step(tag, right, name, j)
        elif tag == "S":
            right_step(tag, squared, name, j)
        elif tag == "L":
            left_step(name, j)
        elif name == "square":
            square(j)
        elif name == "even":
            cube_even()
        else:
            finish()
    for copy in streams.started:
        copy.wait_send()


COPIES = PIECES * (15 + 7 + 7)


def body(block_values, block_columns, block_live):
    return pl.pallas_call(
        kernel,
        name="sign_step",
        out_shape=jax.ShapeDtypeStruct(block_values.shape, jnp.bfloat16),
        in_specs=[
            pl.BlockSpec(memory_space=pltpu.HBM),
            pl.BlockSpec(memory_space=pltpu.HBM),
            pl.BlockSpec(memory_space=pltpu.HBM),
        ],
        out_specs=pl.BlockSpec(memory_space=pltpu.VMEM),
        scratch_shapes=[
            pltpu.VMEM(block_values.shape, jnp.bfloat16),
            pltpu.SMEM((1, ROWS), jnp.int32),
            pltpu.SMEM((1, ROWS), jnp.int32),
            pltpu.VMEM((NC, HEAD + ROWS * BS, BS), jnp.bfloat16),
            pltpu.VMEM((NR, HEAD + ROWS * BS, BS), jnp.bfloat16),
            pltpu.VMEM((NR, ROWS * BS, BS), jnp.bfloat16),
            pltpu.VMEM((NC * BS, BS), jnp.bfloat16),
            pltpu.VMEM((ROWS * BS, BS), jnp.float32),
            pltpu.SemaphoreType.DMA((3,)),
            pltpu.SemaphoreType.DMA((COPIES,)),
            pltpu.SemaphoreType.DMA((COPIES,)),
        ],
        compiler_params=pltpu.CompilerParams(
            collective_id=0, has_side_effects=True, vmem_limit_bytes=28 * 1024 * 1024
        ),
    )(block_values, block_columns.T, block_live.T)


def solution(mesh):
    return jax.shard_map(
        body,
        mesh=mesh,
        in_specs=(P("row", "col", None, None), P("row", "col"), P("row", "col")),
        out_specs=P("row", "col", None, None),
        check_vma=False,
    )
```

```python
import functools

import jax
import jax.numpy as jnp
from jax import lax
from jax.experimental import pallas as pl
from jax.experimental.pallas import tpu as pltpu
from jax.sharding import PartitionSpec as P

MESH = pl.DeviceIdType.MESH
BS = 256
ROWS = 4
HEAD = 16
LEFT_PIECES = 4
LEFT_PIECE = ROWS * BS // LEFT_PIECES
LANES = 128
HALVES = BS // LANES
NR = 8
NC = 16


R, S, L, C = "R", "S", "L", "C"
OWN = "own"
MINUS = "m"
PLUS = "p"
SIDE = "side"
TWO = "two"
SIDE_M = "sideM"
SIDE_P = "sideP"
FAR = "far"
HOP = "hop"
SM = "sm"
SP = "sp"
END = "end"
SQUARE = "square"
EVEN = "even"
FINISH = "finish"

PATHS = {
    ("R", "two"): "--+++-++",
    ("R", "far"): "+-+-yy--",
    ("R", "m"): "zzzyzzzz",
    ("R", "p"): "zzzzyzzy",
    ("S", "two"): "----++-+",
    ("S", "far"): "+--yy-+y",
    ("S", "m"): "yzzzzyyz",
    ("S", "p"): "yzyzyyyz",
    ("L", "two"): "+-++",
    ("L", "far"): "-+--",
}

ORDER = (
    (R, OWN, 0),
    (L, OWN, 1),
    (R, OWN, 2),
    (L, HOP, 0),
    (L, OWN, 0),
    (L, HOP, 1),
    (L, HOP, 3),
    (R, OWN, 1),
    (R, OWN, 3),
    (R, SIDE, 0),
    (L, OWN, 3),
    (R, MINUS, 2),
    (R, SIDE, 2),
    (R, OWN, 4),
    (L, MINUS, 0),
    (L, PLUS, 1),
    (R, PLUS, 1),
    (R, SIDE_M, 0),
    (R, OWN, 7),
    (L, SIDE, 0),
    (L, MINUS, 3),
    (R, TWO, 2),
    (R, OWN, 6),
    (L, SIDE, 1),
    (R, OWN, 5),
    (R, PLUS, 0),
    (R, SIDE, 1),
    (L, HOP, 2),
    (L, SIDE, 3),
    (R, SIDE, 3),
    (R, PLUS, 5),
    (R, TWO, 1),
    (R, MINUS, 1),
    (R, PLUS, 7),
    (R, MINUS, 3),
    (R, SIDE_M, 2),
    (L, SP, 0),
    (R, MINUS, 7),
    (R, PLUS, 2),
    (R, SIDE_P, 1),
    (L, PLUS, 0),
    (R, SIDE_P, 0),
    (R, MINUS, 4),
    (R, MINUS, 6),
    (R, SIDE, 6),
    (R, PLUS, 4),
    (L, SP, 3),
    (R, SIDE_P, 3),
    (R, PLUS, 3),
    (L, SM, 1),
    (R, PLUS, 6),
    (R, TWO, 0),
    (L, MINUS, 1),
    (L, SP, 1),
    (L, TWO, 0),
    (L, PLUS, 3),
    (R, SIDE, 7),
    (R, MINUS, 0),
    (L, OWN, 2),
    (R, MINUS, 5),
    (R, TWO, 3),
    (R, SIDE, 5),
    (R, SIDE_P, 7),
    (L, TWO, 1),
    (R, TWO, 5),
    (R, SIDE_M, 1),
    (L, FAR, 0),
    (L, SM, 0),
    (L, TWO, 3),
    (R, FAR, 2),
    (R, FAR, 0),
    (R, SIDE_P, 6),
    (R, SIDE, 4),
    (L, SIDE, 2),
    (L, SM, 3),
    (R, SIDE_P, 2),
    (R, FAR, 3),
    (R, TWO, 4),
    (L, END, 0),
    (R, SIDE_M, 3),
    (R, FAR, 1),
    (L, FAR, 1),
    (C, SQUARE, 0),
    (S, OWN, 0),
    (L, FAR, 3),
    (R, SIDE_P, 4),
    (R, SIDE_M, 6),
    (L, END, 1),
    (R, TWO, 7),
    (C, SQUARE, 1),
    (S, OWN, 1),
    (L, PLUS, 2),
    (L, END, 3),
    (C, SQUARE, 3),
    (S, OWN, 3),
    (R, TWO, 6),
    (L, MINUS, 2),
    (R, FAR, 5),
    (R, SIDE_M, 7),
    (R, FAR, 7),
    (R, SIDE_P, 5),
    (R, FAR, 4),
    (R, SIDE_M, 5),
    (L, SP, 2),
    (R, SIDE_M, 4),
    (S, PLUS, 0),
    (R, FAR, 6),
    (C, SQUARE, 7),
    (C, SQUARE, 5),
    (S, OWN, 5),
    (S, SIDE, 1),
    (S, SIDE, 0),
    (C, SQUARE, 4),
    (S, MINUS, 0),
    (S, OWN, 4),
    (S, TWO, 0),
    (L, TWO, 2),
    (S, PLUS, 1),
    (L, FAR, 2),
    (S, OWN, 7),
    (S, MINUS, 5),
    (L, SM, 2),
    (S, PLUS, 5),
    (L, END, 2),
    (C, SQUARE, 2),
    (S, OWN, 2),
    (S, SIDE_P, 1),
    (C, SQUARE, 6),
    (S, OWN, 6),
    (S, MINUS, 1),
    (S, MINUS, 7),
    (S, MINUS, 4),
    (S, PLUS, 7),
    (S, SIDE_M, 5),
    (S, PLUS, 3),
    (S, PLUS, 2),
    (S, MINUS, 6),
    (S, SIDE, 3),
    (S, PLUS, 4),
    (S, MINUS, 3),
    (S, TWO, 1),
    (S, SIDE_M, 0),
    (S, SIDE_P, 5),
    (S, TWO, 4),
    (S, SIDE, 6),
    (S, SIDE, 4),
    (S, SIDE_P, 2),
    (S, SIDE_P, 0),
    (S, SIDE_M, 1),
    (S, SIDE, 2),
    (S, TWO, 2),
    (S, TWO, 5),
    (S, TWO, 3),
    (S, TWO, 7),
    (S, FAR, 1),
    (S, SIDE, 5),
    (S, SIDE_M, 6),
    (S, SIDE_M, 3),
    (S, PLUS, 6),
    (S, SIDE, 7),
    (S, FAR, 0),
    (C, EVEN, 0),
    (S, SIDE_P, 4),
    (S, SIDE_P, 3),
    (S, FAR, 5),
    (S, FAR, 4),
    (S, SIDE_M, 4),
    (C, EVEN, 1),
    (S, FAR, 3),
    (S, FAR, 2),
    (S, SIDE_M, 2),
    (S, MINUS, 2),
    (C, FINISH, 0),
    (S, FAR, 6),
    (S, FAR, 7),
    (S, TWO, 6),
    (S, SIDE_M, 7),
    (S, SIDE_P, 7),
    (S, SIDE_P, 6),
    (C, FINISH, 1),
)


class Streams:
    def __init__(self, send_sem, recv_sem):
        self.send_sem, self.recv_sem = send_sem, recv_sem
        self.number = {}
        self.started = []

    def copy(self, key, src, dst, device):
        at = self.number.setdefault(key, len(self.number))
        return pltpu.make_async_remote_copy(
            src_ref=src,
            dst_ref=dst,
            send_sem=self.send_sem.at[at],
            recv_sem=self.recv_sem.at[at],
            device_id=device,
            device_id_type=MESH,
        )

    def send(self, key, src, dst, device):
        copy = self.copy(key, src, dst, device)
        copy.start()
        self.started.append(copy)

    def arrived(self, key, dst, device):
        self.copy(key, dst, dst, device).wait_recv()


def kernel(
    values_in, columns_in, live_in, out, values, columns, live, left, right, squared, chosen, cube, in_sem, send_sem, recv_sem
):
    row, col = lax.axis_index("row"), lax.axis_index("col")
    y_lo, z = row // 4, row % 4
    y_hi, x, core = col // 8, (col // 2) % 4, col % 2

    def row_of(dy, dz):
        return ((y_lo + dy) % 2) * 4 + (z + dz + 4) % 4

    def col_of(dy, dx, dc):
        return (((y_hi + dy) % 2) * 4 + (x + dx + 4) % 4) * 2 + (core + dc) % 2

    near = {
        "y": (row_of(1, 0), col),
        "z+": (row_of(0, 1), col),
        "z-": (row_of(0, -1), col),
        "x+": (row, col_of(0, 1, 0)),
        "x-": (row, col_of(0, -1, 0)),
        "h": (row, col_of(1, 0, 0)),
        "c": (row, col_of(0, 0, 1)),
    }
    barrier = pltpu.get_barrier_semaphore()
    for device in near.values():
        pl.semaphore_signal(barrier, inc=1, device_id=device, device_id_type=MESH)

    fetches = [
        pltpu.make_async_copy(source, target, in_sem.at[at])
        for at, (source, target) in enumerate(
            ((columns_in, columns), (live_in, live), (values_in, values))
        )
    ]
    for fetch in fetches:
        fetch.start()
    for fetch in fetches:
        fetch.wait()

    heads = [
        jnp.broadcast_to(columns[0, j].astype(jnp.float32), (1, BS)) for j in range(ROWS)
    ]
    head = jnp.concatenate(
        heads + [jnp.zeros((HEAD - ROWS, BS), jnp.float32)], axis=0
    ).astype(jnp.bfloat16)
    left[col, 0:HEAD, :] = head
    right[row, 0, 0:HEAD, :] = head[:, 0:LANES]
    for j in range(ROWS):
        block = (values[j, 0].astype(jnp.float32) * live[0, j].astype(jnp.float32)).astype(
            jnp.bfloat16
        )
        left[col, HEAD + j * BS : HEAD + (j + 1) * BS, :] = block
        for h in range(HALVES):
            right[row, h, HEAD + j * BS : HEAD + (j + 1) * BS, :] = block[
                :, h * LANES : (h + 1) * LANES
            ]
    pl.semaphore_wait(barrier, len(near))

    streams = Streams(send_sem, recv_sem)

    def piece(buffer, unit, at):
        if buffer is left:
            if at == 0:
                return left.at[unit, pl.ds(0, HEAD + LEFT_PIECE)]
            return left.at[unit, pl.ds(HEAD + at * LEFT_PIECE, LEFT_PIECE)]
        h, j = at // ROWS, at % ROWS
        if buffer is squared:
            return squared.at[unit, h, pl.ds(j * BS, BS)]
        if at == 0:
            return right.at[unit, 0, pl.ds(0, HEAD + BS)]
        return right.at[unit, h, pl.ds(HEAD + j * BS, BS)]

    def send(name, buffer, unit, j, way):
        ref = piece(buffer, unit, j)
        streams.send((name, j, way), ref, ref, near[way])

    def arrived(name, buffer, unit, j, way):
        streams.arrived((name, j, way), piece(buffer, unit, j), near[way])

    def right_step(tag, buffer, name, j):
        two, far, side_m, side_p = (PATHS[tag, k][j] for k in ("two", "far", "m", "p"))
        if name == OWN:
            for way in ("y", "z+", "z-"):
                send(tag + "own", buffer, row, j, way)
        elif name == MINUS:
            arrived(tag + "own", buffer, row_of(0, -1), j, "z+")
            if two == "+":
                send(tag + "two", buffer, row_of(0, -1), j, "z+")
            if side_m == "y":
                send(tag + "sideM", buffer, row_of(0, -1), j, "y")
        elif name == PLUS:
            arrived(tag + "own", buffer, row_of(0, 1), j, "z-")
            if two == "-":
                send(tag + "two", buffer, row_of(0, 1), j, "z-")
            if side_p == "y":
                send(tag + "sideP", buffer, row_of(0, 1), j, "y")
        elif name == SIDE:
            arrived(tag + "own", buffer, row_of(1, 0), j, "y")
            if side_m == "z":
                send(tag + "sideM", buffer, row_of(1, 0), j, "z+")
            if side_p == "z":
                send(tag + "sideP", buffer, row_of(1, 0), j, "z-")
        elif name == TWO:
            arrived(tag + "two", buffer, row_of(0, 2), j, "z" + two)
            if far == "y":
                send(tag + "far", buffer, row_of(0, 2), j, "y")
        elif name == SIDE_M:
            arrived(tag + "sideM", buffer, row_of(1, -1), j, "z+" if side_m == "z" else "y")
            if far == "+":
                send(tag + "far", buffer, row_of(1, -1), j, "z+")
        elif name == SIDE_P:
            arrived(tag + "sideP", buffer, row_of(1, 1), j, "z-" if side_p == "z" else "y")
            if far == "-":
                send(tag + "far", buffer, row_of(1, 1), j, "z-")
        elif name == FAR:
            arrived(tag + "far", buffer, row_of(1, 2), j, "y" if far == "y" else "z" + far)

    def left_step(name, j):
        two, far = (PATHS["L", k][j] for k in ("two", "far"))
        if name == OWN:
            for way in ("x+", "x-", "c"):
                send("Lown", left, col, j, way)
        elif name == HOP:
            send("Lown", left, col, j, "h")
        elif name == MINUS:
            arrived("Lown", left, col_of(0, -1, 0), j, "x+")
            if two == "+":
                send("Ltwo", left, col_of(0, -1, 0), j, "x+")
            send("Lm", left, col_of(0, -1, 0), j, "c")
        elif name == PLUS:
            arrived("Lown", left, col_of(0, 1, 0), j, "x-")
            if two == "-":
                send("Ltwo", left, col_of(0, 1, 0), j, "x-")
            send("Lp", left, col_of(0, 1, 0), j, "c")
        elif name == SIDE:
            arrived("Lown", left, col_of(1, 0, 0), j, "h")
            for way in ("x+", "x-", "c"):
                send("Lside", left, col_of(1, 0, 0), j, way)
        elif name == SM:
            arrived("Lside", left, col_of(1, -1, 0), j, "x+")
            if far == "+":
                send("Lfar", left, col_of(1, -1, 0), j, "x+")
            send("Lsm", left, col_of(1, -1, 0), j, "c")
        elif name == SP:
            arrived("Lside", left, col_of(1, 1, 0), j, "x-")
            if far == "-":
                send("Lfar", left, col_of(1, 1, 0), j, "x-")
            send("Lsp", left, col_of(1, 1, 0), j, "c")
        elif name == TWO:
            arrived("Ltwo", left, col_of(0, 2, 0), j, "x" + two)
            send("Ltwo", left, col_of(0, 2, 0), j, "c")
        elif name == FAR:
            arrived("Lfar", left, col_of(1, 2, 0), j, "x" + far)
            send("Lfar", left, col_of(1, 2, 0), j, "c")
        elif name == END:
            arrived("Lown", left, col_of(0, 0, 1), j, "c")
            arrived("Lm", left, col_of(0, -1, 1), j, "c")
            arrived("Lp", left, col_of(0, 1, 1), j, "c")
            arrived("Lside", left, col_of(1, 0, 1), j, "c")
            arrived("Lsm", left, col_of(1, -1, 1), j, "c")
            arrived("Lsp", left, col_of(1, 1, 1), j, "c")
            arrived("Ltwo", left, col_of(0, 2, 1), j, "c")
            arrived("Lfar", left, col_of(1, 2, 1), j, "c")

    def select(buffer, first, h, i, parts):
        mine = columns[0, i].astype(jnp.float32)
        alive = (live[0, i] > 0).astype(jnp.float32)
        for r in range(NR):
            right_head = right[r, 0, 0:HEAD, :].astype(jnp.float32)
            for part in parts:
                g = 2 * r + part
                own = left[g, 0:HEAD, 0:LANES].astype(jnp.float32)[i : i + 1]
                weights = []
                for b in range(2):
                    met = right_head[2 * part + b : 2 * part + b + 1]
                    weights.append(
                        jnp.where((own == float(b)) & (met == mine), alive, 0.0).astype(
                            jnp.bfloat16
                        )
                    )
                at = first + 2 * part * BS
                chosen[g * BS : (g + 1) * BS, :] = (
                    buffer[r, h, at : at + BS, :] * weights[0]
                    + buffer[r, h, at + BS : at + 2 * BS, :] * weights[1]
                )

    def product(i, parts):
        groups = [2 * r + part for r in range(NR) for part in parts]
        return jnp.dot(
            jnp.concatenate(
                [left[g, HEAD + i * BS : HEAD + (i + 1) * BS, :] for g in groups], axis=1
            ),
            jnp.concatenate([chosen[g * BS : (g + 1) * BS, :] for g in groups], axis=0),
            preferred_element_type=jnp.float32,
        )

    def square(h, i):
        select(right, HEAD, h, i, (0, 1))
        squared[row, h, i * BS : (i + 1) * BS, :] = product(i, (0, 1)).astype(jnp.bfloat16)

    def cube_even(h):
        for i in range(ROWS):
            select(squared, 0, h, i, (0,))
            cube[h, i * BS : (i + 1) * BS, :] = product(i, (0,))

    def finish(h):
        lanes = slice(h * LANES, (h + 1) * LANES)
        for i in range(ROWS):
            select(squared, 0, h, i, (1,))
            cube_part = cube[h, i * BS : (i + 1) * BS, :] + product(i, (1,))
            masked = left[col, HEAD + i * BS : HEAD + (i + 1) * BS, lanes].astype(jnp.float32)
            out[i, 0, :, lanes] = (1.5 * masked - 0.5 * cube_part).astype(jnp.bfloat16)

    for tag, name, j in ORDER:
        if tag == R:
            right_step(tag, right, name, j)
        elif tag == S:
            right_step(tag, squared, name, j)
        elif tag == L:
            left_step(name, j)
        elif name == SQUARE:
            square(j // ROWS, j % ROWS)
        elif name == EVEN:
            cube_even(j)
        else:
            finish(j)
    for copy in streams.started:
        copy.wait_send()


COPIES = 15 * LEFT_PIECES + (7 + 7) * HALVES * ROWS


def body(block_values, block_columns, block_live):
    return pl.pallas_call(
        kernel,
        name="sign_step",
        out_shape=jax.ShapeDtypeStruct(block_values.shape, jnp.bfloat16),
        in_specs=[
            pl.BlockSpec(memory_space=pltpu.HBM),
            pl.BlockSpec(memory_space=pltpu.HBM),
            pl.BlockSpec(memory_space=pltpu.HBM),
        ],
        out_specs=pl.BlockSpec(memory_space=pltpu.VMEM),
        scratch_shapes=[
            pltpu.VMEM(block_values.shape, jnp.bfloat16),
            pltpu.SMEM((1, ROWS), jnp.int32),
            pltpu.SMEM((1, ROWS), jnp.int32),
            pltpu.VMEM((NC, HEAD + ROWS * BS, BS), jnp.bfloat16),
            pltpu.VMEM((NR, HALVES, HEAD + ROWS * BS, LANES), jnp.bfloat16),
            pltpu.VMEM((NR, HALVES, ROWS * BS, LANES), jnp.bfloat16),
            pltpu.VMEM((NC * BS, LANES), jnp.bfloat16),
            pltpu.VMEM((HALVES, ROWS * BS, LANES), jnp.float32),
            pltpu.SemaphoreType.DMA((3,)),
            pltpu.SemaphoreType.DMA((COPIES,)),
            pltpu.SemaphoreType.DMA((COPIES,)),
        ],
        compiler_params=pltpu.CompilerParams(
            collective_id=0, has_side_effects=True, vmem_limit_bytes=28 * 1024 * 1024
        ),
    )(block_values, block_columns.T, block_live.T)


def solution(mesh):
    return jax.shard_map(
        body,
        mesh=mesh,
        in_specs=(P("row", "col", None, None), P("row", "col"), P("row", "col")),
        out_specs=P("row", "col", None, None),
        check_vma=False,
    )
```

```python
import functools

import jax
import jax.numpy as jnp
from jax import lax
from jax.experimental import pallas as pl
from jax.experimental.pallas import tpu as pltpu
from jax.sharding import PartitionSpec as P

MESH = pl.DeviceIdType.MESH
BS = 256
ROWS = 4
HEAD = 16
LEFT_PIECES = 4
LEFT_PIECE = ROWS * BS // LEFT_PIECES
LANES = 128
HALVES = BS // LANES
NR = 8
NC = 16


R, S, L, C = "R", "S", "L", "C"
OWN = "own"
MINUS = "m"
PLUS = "p"
SIDE = "side"
TWO = "two"
SIDE_M = "sideM"
SIDE_P = "sideP"
FAR = "far"
HOP = "hop"
SM = "sm"
SP = "sp"
END = "end"
SQUARE = "square"
EVEN = "even"
FINISH = "finish"
NEAR = "near"

PATHS = {
    ("R", "two"): "+-++--+-",
    ("R", "far"): "-++---y+",
    ("R", "m"): "zzyzzzzz",
    ("R", "p"): "zzzzzyyy",
    ("S", "two"): "-+---+-+",
    ("S", "far"): "+y+--y+-",
    ("S", "m"): "zzyyzyzy",
    ("S", "p"): "yzyzyyyz",
    ("L", "two"): "+--+",
    ("L", "far"): "-++-",
}

ORDER = (
    (R, OWN, 1),
    (R, OWN, 3),
    (L, OWN, 0),
    (L, HOP, 0),
    (R, OWN, 0),
    (R, OWN, 4),
    (L, OWN, 1),
    (R, SIDE, 1),
    (R, PLUS, 1),
    (L, HOP, 1),
    (L, OWN, 2),
    (L, MINUS, 0),
    (L, HOP, 2),
    (R, OWN, 2),
    (R, SIDE, 3),
    (R, MINUS, 3),
    (R, MINUS, 0),
    (R, PLUS, 3),
    (L, SIDE, 0),
    (R, OWN, 7),
    (R, MINUS, 2),
    (R, PLUS, 4),
    (L, HOP, 3),
    (R, OWN, 6),
    (R, OWN, 5),
    (R, PLUS, 0),
    (L, PLUS, 1),
    (L, SIDE, 1),
    (L, TWO, 0),
    (R, SIDE_P, 3),
    (R, SIDE, 0),
    (L, PLUS, 2),
    (L, SP, 0),
    (L, PLUS, 0),
    (L, MINUS, 1),
    (R, SIDE, 2),
    (L, SIDE, 2),
    (R, MINUS, 6),
    (R, TWO, 3),
    (R, SIDE_M, 1),
    (L, TWO, 1),
    (R, TWO, 1),
    (R, SIDE_M, 2),
    (L, SM, 1),
    (R, SIDE, 7),
    (R, SIDE, 4),
    (R, PLUS, 5),
    (R, TWO, 2),
    (R, MINUS, 5),
    (L, SP, 1),
    (R, SIDE_P, 0),
    (R, SIDE_M, 3),
    (L, SM, 2),
    (L, MINUS, 2),
    (R, PLUS, 7),
    (L, OWN, 3),
    (L, FAR, 0),
    (R, SIDE_P, 4),
    (R, MINUS, 7),
    (L, SM, 0),
    (R, FAR, 1),
    (R, TWO, 6),
    (R, MINUS, 4),
    (R, TWO, 4),
    (L, TWO, 2),
    (R, SIDE, 5),
    (R, SIDE, 6),
    (R, SIDE_P, 5),
    (R, MINUS, 1),
    (R, SIDE_P, 2),
    (R, TWO, 0),
    (L, SIDE, 3),
    (R, FAR, 3),
    (R, PLUS, 6),
    (R, FAR, 0),
    (R, PLUS, 2),
    (L, END, 0),
    (R, SIDE_M, 7),
    (R, SIDE_P, 1),
    (L, FAR, 1),
    (R, FAR, 2),
    (L, SP, 2),
    (R, SIDE_M, 0),
    (C, SQUARE, 0),
    (S, OWN, 0),
    (L, END, 1),
    (L, FAR, 2),
    (R, SIDE_P, 7),
    (C, SQUARE, 1),
    (S, OWN, 1),
    (L, END, 2),
    (C, SQUARE, 2),
    (R, TWO, 5),
    (S, OWN, 2),
    (R, FAR, 4),
    (R, SIDE_M, 5),
    (R, FAR, 5),
    (R, TWO, 7),
    (L, MINUS, 3),
    (S, PLUS, 0),
    (R, SIDE_P, 6),
    (L, PLUS, 3),
    (R, SIDE_M, 6),
    (R, FAR, 6),
    (R, FAR, 7),
    (L, SP, 3),
    (R, SIDE_M, 4),
    (C, SQUARE, 4),
    (S, OWN, 4),
    (C, SQUARE, 5),
    (C, SQUARE, 6),
    (L, SM, 3),
    (S, OWN, 6),
    (S, OWN, 5),
    (S, SIDE, 0),
    (S, MINUS, 2),
    (S, PLUS, 2),
    (S, SIDE, 1),
    (L, TWO, 3),
    (S, MINUS, 1),
    (L, FAR, 3),
    (L, END, 3),
    (C, SQUARE, 3),
    (S, OWN, 3),
    (C, SQUARE, 7),
    (S, OWN, 7),
    (S, PLUS, 4),
    (S, SIDE_M, 1),
    (S, SIDE, 5),
    (S, TWO, 0),
    (S, MINUS, 5),
    (S, SIDE_M, 0),
    (S, TWO, 1),
    (S, SIDE, 3),
    (S, MINUS, 0),
    (S, SIDE, 7),
    (S, PLUS, 5),
    (S, MINUS, 3),
    (S, SIDE, 6),
    (S, PLUS, 3),
    (S, TWO, 4),
    (S, TWO, 5),
    (S, SIDE_M, 5),
    (S, SIDE_M, 2),
    (S, SIDE, 4),
    (S, SIDE_P, 1),
    (S, SIDE_P, 3),
    (S, SIDE_P, 4),
    (S, PLUS, 1),
    (S, SIDE_P, 0),
    (S, PLUS, 7),
    (S, MINUS, 4),
    (S, SIDE_P, 2),
    (S, FAR, 1),
    (S, FAR, 0),
    (C, EVEN, 0),
    (S, PLUS, 6),
    (S, MINUS, 7),
    (S, SIDE_M, 6),
    (S, SIDE_P, 5),
    (S, MINUS, 6),
    (S, FAR, 2),
    (S, TWO, 2),
    (S, SIDE_P, 7),
    (S, SIDE_M, 3),
    (S, TWO, 3),
    (S, SIDE, 2),
    (S, FAR, 3),
    (C, FINISH, 0),
    (S, FAR, 5),
    (S, FAR, 4),
    (S, SIDE_M, 4),
    (C, EVEN, 1),
    (C, NEAR, 1),
    (S, TWO, 7),
    (S, TWO, 6),
    (S, SIDE_P, 6),
    (S, SIDE_M, 7),
    (S, FAR, 6),
    (S, FAR, 7),
    (C, FINISH, 1),
)


class Streams:
    def __init__(self, send_sem, recv_sem):
        self.send_sem, self.recv_sem = send_sem, recv_sem
        self.number = {}
        self.started = []

    def copy(self, key, src, dst, device):
        at = self.number.setdefault(key, len(self.number))
        return pltpu.make_async_remote_copy(
            src_ref=src,
            dst_ref=dst,
            send_sem=self.send_sem.at[at],
            recv_sem=self.recv_sem.at[at],
            device_id=device,
            device_id_type=MESH,
        )

    def send(self, key, src, dst, device):
        copy = self.copy(key, src, dst, device)
        copy.start()
        self.started.append(copy)

    def arrived(self, key, dst, device):
        self.copy(key, dst, dst, device).wait_recv()


def kernel(
    values_in, columns_in, live_in, out, values, columns, live, left, right, squared, chosen, cube, in_sem, send_sem, recv_sem
):
    row, col = lax.axis_index("row"), lax.axis_index("col")
    y_lo, z = row // 4, row % 4
    y_hi, x, core = col // 8, (col // 2) % 4, col % 2

    def row_of(dy, dz):
        return ((y_lo + dy) % 2) * 4 + (z + dz + 4) % 4

    def col_of(dy, dx, dc):
        return (((y_hi + dy) % 2) * 4 + (x + dx + 4) % 4) * 2 + (core + dc) % 2

    near = {
        "y": (row_of(1, 0), col),
        "z+": (row_of(0, 1), col),
        "z-": (row_of(0, -1), col),
        "x+": (row, col_of(0, 1, 0)),
        "x-": (row, col_of(0, -1, 0)),
        "h": (row, col_of(1, 0, 0)),
        "c": (row, col_of(0, 0, 1)),
    }
    barrier = pltpu.get_barrier_semaphore()
    for device in near.values():
        pl.semaphore_signal(barrier, inc=1, device_id=device, device_id_type=MESH)

    fetches = [
        pltpu.make_async_copy(source, target, in_sem.at[at])
        for at, (source, target) in enumerate(
            ((columns_in, columns), (live_in, live), (values_in, values))
        )
    ]
    for fetch in fetches:
        fetch.start()
    for fetch in fetches:
        fetch.wait()

    heads = [
        jnp.broadcast_to(columns[0, j].astype(jnp.float32), (1, BS)) for j in range(ROWS)
    ]
    head = jnp.concatenate(
        heads + [jnp.zeros((HEAD - ROWS, BS), jnp.float32)], axis=0
    ).astype(jnp.bfloat16)
    left[col, 0:HEAD, :] = head
    right[row, 0, 0:HEAD, :] = head[:, 0:LANES]

    def masked_block(j, lanes):
        block = values[j, 0, :, lanes].astype(jnp.float32) * live[0, j].astype(jnp.float32)
        return block.astype(jnp.bfloat16)

    def build_right(h, j):
        lanes = slice(h * LANES, (h + 1) * LANES)
        right[row, h, HEAD + j * BS : HEAD + (j + 1) * BS, :] = masked_block(j, lanes)

    def build_left(j):
        left[col, HEAD + j * BS : HEAD + (j + 1) * BS, :] = masked_block(j, slice(None))

    for j in range(ROWS):
        build_right(0, j)
    pl.semaphore_wait(barrier, len(near))

    streams = Streams(send_sem, recv_sem)

    def piece(buffer, unit, at):
        if buffer is left:
            if at == 0:
                return left.at[unit, pl.ds(0, HEAD + LEFT_PIECE)]
            return left.at[unit, pl.ds(HEAD + at * LEFT_PIECE, LEFT_PIECE)]
        h, j = at // ROWS, at % ROWS
        if buffer is squared:
            return squared.at[unit, h, pl.ds(j * BS, BS)]
        if at == 0:
            return right.at[unit, 0, pl.ds(0, HEAD + BS)]
        return right.at[unit, h, pl.ds(HEAD + j * BS, BS)]

    def send(name, buffer, unit, j, way):
        ref = piece(buffer, unit, j)
        streams.send((name, j, way), ref, ref, near[way])

    def arrived(name, buffer, unit, j, way):
        streams.arrived((name, j, way), piece(buffer, unit, j), near[way])

    def right_step(tag, buffer, name, j):
        two, far, side_m, side_p = (PATHS[tag, k][j] for k in ("two", "far", "m", "p"))
        if name == OWN:
            if tag == R and j >= ROWS:
                build_right(1, j - ROWS)
            for way in ("y", "z+", "z-"):
                send(tag + "own", buffer, row, j, way)
        elif name == MINUS:
            arrived(tag + "own", buffer, row_of(0, -1), j, "z+")
            if two == "+":
                send(tag + "two", buffer, row_of(0, -1), j, "z+")
            if side_m == "y":
                send(tag + "sideM", buffer, row_of(0, -1), j, "y")
        elif name == PLUS:
            arrived(tag + "own", buffer, row_of(0, 1), j, "z-")
            if two == "-":
                send(tag + "two", buffer, row_of(0, 1), j, "z-")
            if side_p == "y":
                send(tag + "sideP", buffer, row_of(0, 1), j, "y")
        elif name == SIDE:
            arrived(tag + "own", buffer, row_of(1, 0), j, "y")
            if side_m == "z":
                send(tag + "sideM", buffer, row_of(1, 0), j, "z+")
            if side_p == "z":
                send(tag + "sideP", buffer, row_of(1, 0), j, "z-")
        elif name == TWO:
            arrived(tag + "two", buffer, row_of(0, 2), j, "z" + two)
            if far == "y":
                send(tag + "far", buffer, row_of(0, 2), j, "y")
        elif name == SIDE_M:
            arrived(tag + "sideM", buffer, row_of(1, -1), j, "z+" if side_m == "z" else "y")
            if far == "+":
                send(tag + "far", buffer, row_of(1, -1), j, "z+")
        elif name == SIDE_P:
            arrived(tag + "sideP", buffer, row_of(1, 1), j, "z-" if side_p == "z" else "y")
            if far == "-":
                send(tag + "far", buffer, row_of(1, 1), j, "z-")
        elif name == FAR:
            arrived(tag + "far", buffer, row_of(1, 2), j, "y" if far == "y" else "z" + far)

    built = set()

    def left_step(name, j):
        two, far = (PATHS["L", k][j] for k in ("two", "far"))
        if name in (OWN, HOP) and j not in built:
            built.add(j)
            build_left(j)
        if name == OWN:
            for way in ("x+", "x-", "c"):
                send("Lown", left, col, j, way)
        elif name == HOP:
            send("Lown", left, col, j, "h")
        elif name == MINUS:
            arrived("Lown", left, col_of(0, -1, 0), j, "x+")
            if two == "+":
                send("Ltwo", left, col_of(0, -1, 0), j, "x+")
            send("Lm", left, col_of(0, -1, 0), j, "c")
        elif name == PLUS:
            arrived("Lown", left, col_of(0, 1, 0), j, "x-")
            if two == "-":
                send("Ltwo", left, col_of(0, 1, 0), j, "x-")
            send("Lp", left, col_of(0, 1, 0), j, "c")
        elif name == SIDE:
            arrived("Lown", left, col_of(1, 0, 0), j, "h")
            for way in ("x+", "x-", "c"):
                send("Lside", left, col_of(1, 0, 0), j, way)
        elif name == SM:
            arrived("Lside", left, col_of(1, -1, 0), j, "x+")
            if far == "+":
                send("Lfar", left, col_of(1, -1, 0), j, "x+")
            send("Lsm", left, col_of(1, -1, 0), j, "c")
        elif name == SP:
            arrived("Lside", left, col_of(1, 1, 0), j, "x-")
            if far == "-":
                send("Lfar", left, col_of(1, 1, 0), j, "x-")
            send("Lsp", left, col_of(1, 1, 0), j, "c")
        elif name == TWO:
            arrived("Ltwo", left, col_of(0, 2, 0), j, "x" + two)
            send("Ltwo", left, col_of(0, 2, 0), j, "c")
        elif name == FAR:
            arrived("Lfar", left, col_of(1, 2, 0), j, "x" + far)
            send("Lfar", left, col_of(1, 2, 0), j, "c")
        elif name == END:
            arrived("Lown", left, col_of(0, 0, 1), j, "c")
            arrived("Lm", left, col_of(0, -1, 1), j, "c")
            arrived("Lp", left, col_of(0, 1, 1), j, "c")
            arrived("Lside", left, col_of(1, 0, 1), j, "c")
            arrived("Lsm", left, col_of(1, -1, 1), j, "c")
            arrived("Lsp", left, col_of(1, 1, 1), j, "c")
            arrived("Ltwo", left, col_of(0, 2, 1), j, "c")
            arrived("Lfar", left, col_of(1, 2, 1), j, "c")

    def select(buffer, first, h, i, groups):
        mine = columns[0, i].astype(jnp.float32)
        alive = (live[0, i] > 0).astype(jnp.float32)
        for slot, (r, part) in enumerate(groups):
            right_head = right[r, 0, 0:HEAD, :].astype(jnp.float32)
            own = left[2 * r + part, 0:HEAD, 0:LANES].astype(jnp.float32)[i : i + 1]
            weights = []
            for b in range(2):
                met = right_head[2 * part + b : 2 * part + b + 1]
                weights.append(
                    jnp.where((own == float(b)) & (met == mine), alive, 0.0).astype(jnp.bfloat16)
                )
            at = first + 2 * part * BS
            chosen[slot * BS : (slot + 1) * BS, :] = (
                buffer[r, h, at : at + BS, :] * weights[0]
                + buffer[r, h, at + BS : at + 2 * BS, :] * weights[1]
            )

    def product(i, groups):
        return jnp.dot(
            jnp.concatenate(
                [
                    left[2 * r + part, HEAD + i * BS : HEAD + (i + 1) * BS, :]
                    for r, part in groups
                ],
                axis=1,
            ),
            chosen[0 : len(groups) * BS, :],
            preferred_element_type=jnp.float32,
        )

    both = [(r, part) for r in range(NR) for part in range(2)]
    even = [(r, 0) for r in range(NR)]
    odd = [(r, 1) for r in range(NR)]
    odd_near = [(row_of(dy, dz), 1) for dy, dz in ((0, 0), (1, 0), (0, -1), (0, 1))]
    odd_far = [(row_of(dy, dz), 1) for dy, dz in ((0, 2), (1, -1), (1, 1), (1, 2))]

    def square(h, i):
        select(right, HEAD, h, i, both)
        squared[row, h, i * BS : (i + 1) * BS, :] = product(i, both).astype(jnp.bfloat16)

    def cube_even(h):
        for i in range(ROWS):
            select(squared, 0, h, i, even)
            cube[h, i * BS : (i + 1) * BS, :] = product(i, even)

    def cube_near(h):
        for i in range(ROWS):
            select(squared, 0, h, i, odd_near)
            cube[h, i * BS : (i + 1) * BS, :] += product(i, odd_near)

    def finish(h):
        groups = odd_far if h == HALVES - 1 else odd
        lanes = slice(h * LANES, (h + 1) * LANES)
        for i in range(ROWS):
            select(squared, 0, h, i, groups)
            cube_part = cube[h, i * BS : (i + 1) * BS, :] + product(i, groups)
            masked = left[col, HEAD + i * BS : HEAD + (i + 1) * BS, lanes].astype(jnp.float32)
            out[i, 0, :, lanes] = (1.5 * masked - 0.5 * cube_part).astype(jnp.bfloat16)

    for tag, name, j in ORDER:
        if tag == R:
            right_step(tag, right, name, j)
        elif tag == S:
            right_step(tag, squared, name, j)
        elif tag == L:
            left_step(name, j)
        elif name == SQUARE:
            square(j // ROWS, j % ROWS)
        elif name == EVEN:
            cube_even(j)
        elif name == NEAR:
            cube_near(j)
        else:
            finish(j)
    for copy in streams.started:
        copy.wait_send()


COPIES = 15 * LEFT_PIECES + (7 + 7) * HALVES * ROWS


def body(block_values, block_columns, block_live):
    return pl.pallas_call(
        kernel,
        name="sign_step",
        out_shape=jax.ShapeDtypeStruct(block_values.shape, jnp.bfloat16),
        in_specs=[
            pl.BlockSpec(memory_space=pltpu.HBM),
            pl.BlockSpec(memory_space=pltpu.HBM),
            pl.BlockSpec(memory_space=pltpu.HBM),
        ],
        out_specs=pl.BlockSpec(memory_space=pltpu.VMEM),
        scratch_shapes=[
            pltpu.VMEM(block_values.shape, jnp.bfloat16),
            pltpu.SMEM((1, ROWS), jnp.int32),
            pltpu.SMEM((1, ROWS), jnp.int32),
            pltpu.VMEM((NC, HEAD + ROWS * BS, BS), jnp.bfloat16),
            pltpu.VMEM((NR, HALVES, HEAD + ROWS * BS, LANES), jnp.bfloat16),
            pltpu.VMEM((NR, HALVES, ROWS * BS, LANES), jnp.bfloat16),
            pltpu.VMEM((NC * BS, LANES), jnp.bfloat16),
            pltpu.VMEM((HALVES, ROWS * BS, LANES), jnp.float32),
            pltpu.SemaphoreType.DMA((3,)),
            pltpu.SemaphoreType.DMA((COPIES,)),
            pltpu.SemaphoreType.DMA((COPIES,)),
        ],
        compiler_params=pltpu.CompilerParams(
            collective_id=0, has_side_effects=True, vmem_limit_bytes=28 * 1024 * 1024
        ),
    )(block_values, block_columns.T, block_live.T)


def solution(mesh):
    return jax.shard_map(
        body,
        mesh=mesh,
        in_specs=(P("row", "col", None, None), P("row", "col"), P("row", "col")),
        out_specs=P("row", "col", None, None),
        check_vma=False,
    )
```

```python
import functools

import jax
import jax.numpy as jnp
from jax import lax
from jax.experimental import pallas as pl
from jax.experimental.pallas import tpu as pltpu
from jax.sharding import PartitionSpec as P

MESH = pl.DeviceIdType.MESH
BS = 256
ROWS = 4
HEAD = 16
LEFT_PIECES = 4
LEFT_PIECE = ROWS * BS // LEFT_PIECES
LANES = 128
HALVES = BS // LANES
NR = 8
NC = 16


R, S, L, C = "R", "S", "L", "C"
OWN = "own"
MINUS = "m"
PLUS = "p"
SIDE = "side"
TWO = "two"
SIDE_M = "sideM"
SIDE_P = "sideP"
FAR = "far"
HOP = "hop"
SM = "sm"
SP = "sp"
END = "end"
SQUARE = "square"
EVEN = "even"
FINISH = "finish"
NEAR = "near"

PATHS = {
    ("R", "two"): "+-++--+-",
    ("R", "far"): "-++---y+",
    ("R", "m"): "zzyzzzzz",
    ("R", "p"): "zzzzzyyy",
    ("S", "two"): "-+---+-+",
    ("S", "far"): "+y+--y+-",
    ("S", "m"): "zzyyzyzy",
    ("S", "p"): "yzyzyyyz",
    ("L", "two"): "+--+",
    ("L", "far"): "-++-",
}

ORDER = (
    (R, OWN, 1),
    (R, OWN, 3),
    (L, OWN, 0),
    (L, HOP, 0),
    (R, OWN, 0),
    (R, OWN, 4),
    (L, OWN, 1),
    (R, SIDE, 1),
    (R, PLUS, 1),
    (L, HOP, 1),
    (L, OWN, 2),
    (L, MINUS, 0),
    (L, HOP, 2),
    (R, OWN, 2),
    (R, SIDE, 3),
    (R, MINUS, 3),
    (R, MINUS, 0),
    (R, PLUS, 3),
    (L, SIDE, 0),
    (R, OWN, 7),
    (R, MINUS, 2),
    (R, PLUS, 4),
    (L, HOP, 3),
    (R, OWN, 6),
    (R, OWN, 5),
    (R, PLUS, 0),
    (L, PLUS, 1),
    (L, SIDE, 1),
    (L, TWO, 0),
    (R, SIDE_P, 3),
    (R, SIDE, 0),
    (L, PLUS, 2),
    (L, SP, 0),
    (L, PLUS, 0),
    (L, MINUS, 1),
    (R, SIDE, 2),
    (L, SIDE, 2),
    (R, MINUS, 6),
    (R, TWO, 3),
    (R, SIDE_M, 1),
    (L, TWO, 1),
    (R, TWO, 1),
    (R, SIDE_M, 2),
    (L, SM, 1),
    (R, SIDE, 7),
    (R, SIDE, 4),
    (R, PLUS, 5),
    (R, TWO, 2),
    (R, MINUS, 5),
    (L, SP, 1),
    (R, SIDE_P, 0),
    (R, SIDE_M, 3),
    (L, SM, 2),
    (L, MINUS, 2),
    (R, PLUS, 7),
    (L, OWN, 3),
    (L, FAR, 0),
    (R, SIDE_P, 4),
    (R, MINUS, 7),
    (L, SM, 0),
    (R, FAR, 1),
    (R, TWO, 6),
    (R, MINUS, 4),
    (R, TWO, 4),
    (L, TWO, 2),
    (R, SIDE, 5),
    (R, SIDE, 6),
    (R, SIDE_P, 5),
    (R, MINUS, 1),
    (R, SIDE_P, 2),
    (R, TWO, 0),
    (L, SIDE, 3),
    (R, FAR, 3),
    (R, PLUS, 6),
    (R, FAR, 0),
    (R, PLUS, 2),
    (L, END, 0),
    (R, SIDE_M, 7),
    (R, SIDE_P, 1),
    (L, FAR, 1),
    (R, FAR, 2),
    (L, SP, 2),
    (R, SIDE_M, 0),
    (C, SQUARE, 0),
    (S, OWN, 0),
    (L, END, 1),
    (L, FAR, 2),
    (R, SIDE_P, 7),
    (C, SQUARE, 1),
    (S, OWN, 1),
    (L, END, 2),
    (C, SQUARE, 2),
    (R, TWO, 5),
    (S, OWN, 2),
    (R, FAR, 4),
    (R, SIDE_M, 5),
    (R, FAR, 5),
    (R, TWO, 7),
    (L, MINUS, 3),
    (S, PLUS, 0),
    (R, SIDE_P, 6),
    (L, PLUS, 3),
    (R, SIDE_M, 6),
    (R, FAR, 6),
    (R, FAR, 7),
    (L, SP, 3),
    (R, SIDE_M, 4),
    (C, SQUARE, 4),
    (S, OWN, 4),
    (C, SQUARE, 5),
    (C, SQUARE, 6),
    (L, SM, 3),
    (S, OWN, 6),
    (S, OWN, 5),
    (S, SIDE, 0),
    (S, MINUS, 2),
    (S, PLUS, 2),
    (S, SIDE, 1),
    (L, TWO, 3),
    (S, MINUS, 1),
    (L, FAR, 3),
    (L, END, 3),
    (C, SQUARE, 3),
    (S, OWN, 3),
    (C, SQUARE, 7),
    (S, OWN, 7),
    (S, PLUS, 4),
    (S, SIDE_M, 1),
    (S, SIDE, 5),
    (S, TWO, 0),
    (S, MINUS, 5),
    (S, SIDE_M, 0),
    (S, TWO, 1),
    (S, SIDE, 3),
    (S, MINUS, 0),
    (S, SIDE, 7),
    (S, PLUS, 5),
    (S, MINUS, 3),
    (S, SIDE, 6),
    (S, PLUS, 3),
    (S, TWO, 4),
    (S, TWO, 5),
    (S, SIDE_M, 5),
    (S, SIDE_M, 2),
    (S, SIDE, 4),
    (S, SIDE_P, 1),
    (S, SIDE_P, 3),
    (S, SIDE_P, 4),
    (S, PLUS, 1),
    (S, SIDE_P, 0),
    (S, PLUS, 7),
    (S, MINUS, 4),
    (S, SIDE_P, 2),
    (S, FAR, 1),
    (S, FAR, 0),
    (C, EVEN, 0),
    (S, PLUS, 6),
    (S, MINUS, 7),
    (S, SIDE_M, 6),
    (S, SIDE_P, 5),
    (S, MINUS, 6),
    (S, FAR, 2),
    (S, TWO, 2),
    (S, SIDE_P, 7),
    (S, SIDE_M, 3),
    (S, TWO, 3),
    (S, SIDE, 2),
    (S, FAR, 3),
    (C, FINISH, 0),
    (S, FAR, 5),
    (S, FAR, 4),
    (S, SIDE_M, 4),
    (C, EVEN, 1),
    (C, NEAR, 1),
    (S, TWO, 7),
    (S, TWO, 6),
    (S, SIDE_P, 6),
    (S, SIDE_M, 7),
    (S, FAR, 6),
    (S, FAR, 7),
    (C, FINISH, 1),
)


class Streams:
    def __init__(self, send_sem, recv_sem):
        self.send_sem, self.recv_sem = send_sem, recv_sem
        self.number = {}
        self.started = []

    def copy(self, key, src, dst, device):
        at = self.number.setdefault(key, len(self.number))
        return pltpu.make_async_remote_copy(
            src_ref=src,
            dst_ref=dst,
            send_sem=self.send_sem.at[at],
            recv_sem=self.recv_sem.at[at],
            device_id=device,
            device_id_type=MESH,
        )

    def send(self, key, src, dst, device):
        copy = self.copy(key, src, dst, device)
        copy.start()
        self.started.append(copy)

    def arrived(self, key, dst, device):
        self.copy(key, dst, dst, device).wait_recv()


def kernel(
    values_in, columns_in, live_in, out, values, columns, live, left, right, squared, chosen, cube, in_sem, send_sem, recv_sem
):
    row, col = lax.axis_index("row"), lax.axis_index("col")
    y_lo, z = row // 4, row % 4
    y_hi, x, core = col // 8, (col // 2) % 4, col % 2

    def row_of(dy, dz):
        return ((y_lo + dy) % 2) * 4 + (z + dz + 4) % 4

    def col_of(dy, dx, dc):
        return (((y_hi + dy) % 2) * 4 + (x + dx + 4) % 4) * 2 + (core + dc) % 2

    near = {
        "y": (row_of(1, 0), col),
        "z+": (row_of(0, 1), col),
        "z-": (row_of(0, -1), col),
        "x+": (row, col_of(0, 1, 0)),
        "x-": (row, col_of(0, -1, 0)),
        "h": (row, col_of(1, 0, 0)),
        "c": (row, col_of(0, 0, 1)),
    }
    barrier = pltpu.get_barrier_semaphore()
    for device in near.values():
        pl.semaphore_signal(barrier, inc=1, device_id=device, device_id_type=MESH)

    fetches = [
        pltpu.make_async_copy(source, target, in_sem.at[at])
        for at, (source, target) in enumerate(
            [(columns_in, columns), (live_in, live)]
            + [(values_in.at[j], values.at[j]) for j in range(ROWS)]
        )
    ]
    for fetch in fetches:
        fetch.start()
    for fetch in fetches[:2]:
        fetch.wait()

    heads = [
        jnp.broadcast_to(columns[0, j].astype(jnp.float32), (1, BS)) for j in range(ROWS)
    ]
    head = jnp.concatenate(
        heads + [jnp.zeros((HEAD - ROWS, BS), jnp.float32)], axis=0
    ).astype(jnp.bfloat16)
    left[col, 0:HEAD, :] = head
    right[row, 0, 0:HEAD, :] = head[:, 0:LANES]

    def masked_block(j, lanes):
        block = values[j, 0, :, lanes].astype(jnp.float32) * live[0, j].astype(jnp.float32)
        return block.astype(jnp.bfloat16)

    def build_right(h, j):
        lanes = slice(h * LANES, (h + 1) * LANES)
        right[row, h, HEAD + j * BS : HEAD + (j + 1) * BS, :] = masked_block(j, lanes)

    def build_left(j):
        left[col, HEAD + j * BS : HEAD + (j + 1) * BS, :] = masked_block(j, slice(None))

    for j in range(ROWS):
        fetches[2 + j].wait()
        build_right(0, j)
    pl.semaphore_wait(barrier, len(near))

    streams = Streams(send_sem, recv_sem)

    def piece(buffer, unit, at):
        if buffer is left:
            if at == 0:
                return left.at[unit, pl.ds(0, HEAD + LEFT_PIECE)]
            return left.at[unit, pl.ds(HEAD + at * LEFT_PIECE, LEFT_PIECE)]
        h, j = at // ROWS, at % ROWS
        if buffer is squared:
            return squared.at[unit, h, pl.ds(j * BS, BS)]
        if at == 0:
            return right.at[unit, 0, pl.ds(0, HEAD + BS)]
        return right.at[unit, h, pl.ds(HEAD + j * BS, BS)]

    def send(name, buffer, unit, j, way):
        ref = piece(buffer, unit, j)
        streams.send((name, j, way), ref, ref, near[way])

    def arrived(name, buffer, unit, j, way):
        streams.arrived((name, j, way), piece(buffer, unit, j), near[way])

    def right_step(tag, buffer, name, j):
        two, far, side_m, side_p = (PATHS[tag, k][j] for k in ("two", "far", "m", "p"))
        if name == OWN:
            if tag == R and j >= ROWS:
                build_right(1, j - ROWS)
            for way in ("y", "z+", "z-"):
                send(tag + "own", buffer, row, j, way)
        elif name == MINUS:
            arrived(tag + "own", buffer, row_of(0, -1), j, "z+")
            if two == "+":
                send(tag + "two", buffer, row_of(0, -1), j, "z+")
            if side_m == "y":
                send(tag + "sideM", buffer, row_of(0, -1), j, "y")
        elif name == PLUS:
            arrived(tag + "own", buffer, row_of(0, 1), j, "z-")
            if two == "-":
                send(tag + "two", buffer, row_of(0, 1), j, "z-")
            if side_p == "y":
                send(tag + "sideP", buffer, row_of(0, 1), j, "y")
        elif name == SIDE:
            arrived(tag + "own", buffer, row_of(1, 0), j, "y")
            if side_m == "z":
                send(tag + "sideM", buffer, row_of(1, 0), j, "z+")
            if side_p == "z":
                send(tag + "sideP", buffer, row_of(1, 0), j, "z-")
        elif name == TWO:
            arrived(tag + "two", buffer, row_of(0, 2), j, "z" + two)
            if far == "y":
                send(tag + "far", buffer, row_of(0, 2), j, "y")
        elif name == SIDE_M:
            arrived(tag + "sideM", buffer, row_of(1, -1), j, "z+" if side_m == "z" else "y")
            if far == "+":
                send(tag + "far", buffer, row_of(1, -1), j, "z+")
        elif name == SIDE_P:
            arrived(tag + "sideP", buffer, row_of(1, 1), j, "z-" if side_p == "z" else "y")
            if far == "-":
                send(tag + "far", buffer, row_of(1, 1), j, "z-")
        elif name == FAR:
            arrived(tag + "far", buffer, row_of(1, 2), j, "y" if far == "y" else "z" + far)

    built = set()

    def left_step(name, j):
        two, far = (PATHS["L", k][j] for k in ("two", "far"))
        if name in (OWN, HOP) and j not in built:
            built.add(j)
            build_left(j)
        if name == OWN:
            for way in ("x+", "x-", "c"):
                send("Lown", left, col, j, way)
        elif name == HOP:
            send("Lown", left, col, j, "h")
        elif name == MINUS:
            arrived("Lown", left, col_of(0, -1, 0), j, "x+")
            if two == "+":
                send("Ltwo", left, col_of(0, -1, 0), j, "x+")
            send("Lm", left, col_of(0, -1, 0), j, "c")
        elif name == PLUS:
            arrived("Lown", left, col_of(0, 1, 0), j, "x-")
            if two == "-":
                send("Ltwo", left, col_of(0, 1, 0), j, "x-")
            send("Lp", left, col_of(0, 1, 0), j, "c")
        elif name == SIDE:
            arrived("Lown", left, col_of(1, 0, 0), j, "h")
            for way in ("x+", "x-", "c"):
                send("Lside", left, col_of(1, 0, 0), j, way)
        elif name == SM:
            arrived("Lside", left, col_of(1, -1, 0), j, "x+")
            if far == "+":
                send("Lfar", left, col_of(1, -1, 0), j, "x+")
            send("Lsm", left, col_of(1, -1, 0), j, "c")
        elif name == SP:
            arrived("Lside", left, col_of(1, 1, 0), j, "x-")
            if far == "-":
                send("Lfar", left, col_of(1, 1, 0), j, "x-")
            send("Lsp", left, col_of(1, 1, 0), j, "c")
        elif name == TWO:
            arrived("Ltwo", left, col_of(0, 2, 0), j, "x" + two)
            send("Ltwo", left, col_of(0, 2, 0), j, "c")
        elif name == FAR:
            arrived("Lfar", left, col_of(1, 2, 0), j, "x" + far)
            send("Lfar", left, col_of(1, 2, 0), j, "c")
        elif name == END:
            arrived("Lown", left, col_of(0, 0, 1), j, "c")
            arrived("Lm", left, col_of(0, -1, 1), j, "c")
            arrived("Lp", left, col_of(0, 1, 1), j, "c")
            arrived("Lside", left, col_of(1, 0, 1), j, "c")
            arrived("Lsm", left, col_of(1, -1, 1), j, "c")
            arrived("Lsp", left, col_of(1, 1, 1), j, "c")
            arrived("Ltwo", left, col_of(0, 2, 1), j, "c")
            arrived("Lfar", left, col_of(1, 2, 1), j, "c")

    def select(buffer, first, h, i, groups):
        mine = columns[0, i].astype(jnp.float32)
        alive = (live[0, i] > 0).astype(jnp.float32)
        for slot, (r, part) in enumerate(groups):
            right_head = right[r, 0, 0:HEAD, :].astype(jnp.float32)
            own = left[2 * r + part, 0:HEAD, 0:LANES].astype(jnp.float32)[i : i + 1]
            weights = []
            for b in range(2):
                met = right_head[2 * part + b : 2 * part + b + 1]
                weights.append(
                    jnp.where((own == float(b)) & (met == mine), alive, 0.0).astype(jnp.bfloat16)
                )
            at = first + 2 * part * BS
            chosen[slot * BS : (slot + 1) * BS, :] = (
                buffer[r, h, at : at + BS, :] * weights[0]
                + buffer[r, h, at + BS : at + 2 * BS, :] * weights[1]
            )

    def product(i, groups):
        return jnp.dot(
            jnp.concatenate(
                [
                    left[2 * r + part, HEAD + i * BS : HEAD + (i + 1) * BS, :]
                    for r, part in groups
                ],
                axis=1,
            ),
            chosen[0 : len(groups) * BS, :],
            preferred_element_type=jnp.float32,
        )

    both = [(r, part) for r in range(NR) for part in range(2)]
    even = [(r, 0) for r in range(NR)]
    odd = [(r, 1) for r in range(NR)]
    odd_near = [(row_of(dy, dz), 1) for dy, dz in ((0, 0), (1, 0), (0, -1), (0, 1))]
    odd_far = [(row_of(dy, dz), 1) for dy, dz in ((0, 2), (1, -1), (1, 1), (1, 2))]

    def square(h, i):
        select(right, HEAD, h, i, both)
        squared[row, h, i * BS : (i + 1) * BS, :] = product(i, both).astype(jnp.bfloat16)

    def cube_even(h):
        for i in range(ROWS):
            select(squared, 0, h, i, even)
            cube[h, i * BS : (i + 1) * BS, :] = product(i, even)

    def cube_near(h):
        for i in range(ROWS):
            select(squared, 0, h, i, odd_near)
            cube[h, i * BS : (i + 1) * BS, :] += product(i, odd_near)

    def finish(h):
        groups = odd_far if h == HALVES - 1 else odd
        lanes = slice(h * LANES, (h + 1) * LANES)
        for i in range(ROWS):
            select(squared, 0, h, i, groups)
            cube_part = cube[h, i * BS : (i + 1) * BS, :] + product(i, groups)
            masked = left[col, HEAD + i * BS : HEAD + (i + 1) * BS, lanes].astype(jnp.float32)
            out[i, 0, :, lanes] = (1.5 * masked - 0.5 * cube_part).astype(jnp.bfloat16)

    for tag, name, j in ORDER:
        if tag == R:
            right_step(tag, right, name, j)
        elif tag == S:
            right_step(tag, squared, name, j)
        elif tag == L:
            left_step(name, j)
        elif name == SQUARE:
            square(j // ROWS, j % ROWS)
        elif name == EVEN:
            cube_even(j)
        elif name == NEAR:
            cube_near(j)
        else:
            finish(j)
    for copy in streams.started:
        copy.wait_send()


COPIES = 15 * LEFT_PIECES + (7 + 7) * HALVES * ROWS


def body(block_values, block_columns, block_live):
    return pl.pallas_call(
        kernel,
        name="sign_step",
        out_shape=jax.ShapeDtypeStruct(block_values.shape, jnp.bfloat16),
        in_specs=[
            pl.BlockSpec(memory_space=pltpu.HBM),
            pl.BlockSpec(memory_space=pltpu.HBM),
            pl.BlockSpec(memory_space=pltpu.HBM),
        ],
        out_specs=pl.BlockSpec(memory_space=pltpu.VMEM),
        scratch_shapes=[
            pltpu.VMEM(block_values.shape, jnp.bfloat16),
            pltpu.SMEM((1, ROWS), jnp.int32),
            pltpu.SMEM((1, ROWS), jnp.int32),
            pltpu.VMEM((NC, HEAD + ROWS * BS, BS), jnp.bfloat16),
            pltpu.VMEM((NR, HALVES, HEAD + ROWS * BS, LANES), jnp.bfloat16),
            pltpu.VMEM((NR, HALVES, ROWS * BS, LANES), jnp.bfloat16),
            pltpu.VMEM((NC * BS, LANES), jnp.bfloat16),
            pltpu.VMEM((HALVES, ROWS * BS, LANES), jnp.float32),
            pltpu.SemaphoreType.DMA((2 + ROWS,)),
            pltpu.SemaphoreType.DMA((COPIES,)),
            pltpu.SemaphoreType.DMA((COPIES,)),
        ],
        compiler_params=pltpu.CompilerParams(
            collective_id=0, has_side_effects=True, vmem_limit_bytes=28 * 1024 * 1024
        ),
    )(block_values, block_columns.T, block_live.T)


def solution(mesh):
    return jax.shard_map(
        body,
        mesh=mesh,
        in_specs=(P("row", "col", None, None), P("row", "col"), P("row", "col")),
        out_specs=P("row", "col", None, None),
        check_vma=False,
    )
```

```python
import functools

import jax
import jax.numpy as jnp
from jax import lax
from jax.experimental import pallas as pl
from jax.experimental.pallas import tpu as pltpu
from jax.sharding import PartitionSpec as P

MESH = pl.DeviceIdType.MESH
BS = 256
ROWS = 4
HEAD = 16
LEFT_PIECES = 4
LEFT_PIECE = ROWS * BS // LEFT_PIECES
LANES = 128
HALVES = BS // LANES
NR = 8
NC = 16


R, S, L, C = "R", "S", "L", "C"
OWN = "own"
MINUS = "m"
PLUS = "p"
SIDE = "side"
TWO = "two"
SIDE_M = "sideM"
SIDE_P = "sideP"
FAR = "far"
HOP = "hop"
SM = "sm"
SP = "sp"
END = "end"
SQUARE = "square"
EVEN = "even"
FINISH = "finish"
NEAR = "near"

PATHS = {
    ("R", "two"): "+-++--+-",
    ("R", "far"): "-++---y+",
    ("R", "m"): "zzyzzzzz",
    ("R", "p"): "zzzzzyyy",
    ("S", "two"): "-+---+-+",
    ("S", "far"): "+y+--y+-",
    ("S", "m"): "zzyyzyzy",
    ("S", "p"): "yzyzyyyz",
    ("L", "two"): "+--+",
    ("L", "far"): "-++-",
}

ORDER = (
    (R, OWN, 1),
    (R, OWN, 3),
    (L, OWN, 0),
    (L, HOP, 0),
    (R, OWN, 0),
    (R, OWN, 4),
    (L, OWN, 1),
    (R, SIDE, 1),
    (R, PLUS, 1),
    (L, HOP, 1),
    (L, OWN, 2),
    (L, MINUS, 0),
    (L, HOP, 2),
    (R, OWN, 2),
    (R, SIDE, 3),
    (R, MINUS, 3),
    (R, MINUS, 0),
    (R, PLUS, 3),
    (L, SIDE, 0),
    (R, OWN, 7),
    (R, MINUS, 2),
    (R, PLUS, 4),
    (L, HOP, 3),
    (R, OWN, 6),
    (R, OWN, 5),
    (R, PLUS, 0),
    (L, PLUS, 1),
    (L, SIDE, 1),
    (L, TWO, 0),
    (R, SIDE_P, 3),
    (R, SIDE, 0),
    (L, PLUS, 2),
    (L, SP, 0),
    (L, PLUS, 0),
    (L, MINUS, 1),
    (R, SIDE, 2),
    (L, SIDE, 2),
    (R, MINUS, 6),
    (R, TWO, 3),
    (R, SIDE_M, 1),
    (L, TWO, 1),
    (R, TWO, 1),
    (R, SIDE_M, 2),
    (L, SM, 1),
    (R, SIDE, 7),
    (R, SIDE, 4),
    (R, PLUS, 5),
    (R, TWO, 2),
    (R, MINUS, 5),
    (L, SP, 1),
    (R, SIDE_P, 0),
    (R, SIDE_M, 3),
    (L, SM, 2),
    (L, MINUS, 2),
    (R, PLUS, 7),
    (L, OWN, 3),
    (L, FAR, 0),
    (R, SIDE_P, 4),
    (R, MINUS, 7),
    (L, SM, 0),
    (R, FAR, 1),
    (R, TWO, 6),
    (R, MINUS, 4),
    (R, TWO, 4),
    (L, TWO, 2),
    (R, SIDE, 5),
    (R, SIDE, 6),
    (R, SIDE_P, 5),
    (R, MINUS, 1),
    (R, SIDE_P, 2),
    (R, TWO, 0),
    (L, SIDE, 3),
    (R, FAR, 3),
    (R, PLUS, 6),
    (R, FAR, 0),
    (R, PLUS, 2),
    (L, END, 0),
    (R, SIDE_M, 7),
    (R, SIDE_P, 1),
    (L, FAR, 1),
    (R, FAR, 2),
    (L, SP, 2),
    (R, SIDE_M, 0),
    (C, SQUARE, 0),
    (S, OWN, 0),
    (L, END, 1),
    (L, FAR, 2),
    (R, SIDE_P, 7),
    (C, SQUARE, 1),
    (S, OWN, 1),
    (L, END, 2),
    (C, SQUARE, 2),
    (R, TWO, 5),
    (S, OWN, 2),
    (R, FAR, 4),
    (R, SIDE_M, 5),
    (R, FAR, 5),
    (R, TWO, 7),
    (L, MINUS, 3),
    (S, PLUS, 0),
    (R, SIDE_P, 6),
    (L, PLUS, 3),
    (R, SIDE_M, 6),
    (R, FAR, 6),
    (R, FAR, 7),
    (L, SP, 3),
    (R, SIDE_M, 4),
    (C, SQUARE, 4),
    (S, OWN, 4),
    (C, SQUARE, 5),
    (C, SQUARE, 6),
    (L, SM, 3),
    (S, OWN, 6),
    (S, OWN, 5),
    (S, SIDE, 0),
    (S, MINUS, 2),
    (S, PLUS, 2),
    (S, SIDE, 1),
    (L, TWO, 3),
    (S, MINUS, 1),
    (L, FAR, 3),
    (L, END, 3),
    (C, SQUARE, 3),
    (S, OWN, 3),
    (C, SQUARE, 7),
    (S, OWN, 7),
    (S, PLUS, 4),
    (S, SIDE_M, 1),
    (S, SIDE, 5),
    (S, TWO, 0),
    (S, MINUS, 5),
    (S, SIDE_M, 0),
    (S, TWO, 1),
    (S, SIDE, 3),
    (S, MINUS, 0),
    (S, SIDE, 7),
    (S, PLUS, 5),
    (S, MINUS, 3),
    (S, SIDE, 6),
    (S, PLUS, 3),
    (S, TWO, 4),
    (S, TWO, 5),
    (S, SIDE_M, 5),
    (S, SIDE_M, 2),
    (S, SIDE, 4),
    (S, SIDE_P, 1),
    (S, SIDE_P, 3),
    (S, SIDE_P, 4),
    (S, PLUS, 1),
    (S, SIDE_P, 0),
    (S, PLUS, 7),
    (S, MINUS, 4),
    (S, SIDE_P, 2),
    (S, FAR, 1),
    (S, FAR, 0),
    (C, EVEN, 0),
    (S, PLUS, 6),
    (S, MINUS, 7),
    (S, SIDE_M, 6),
    (S, SIDE_P, 5),
    (S, MINUS, 6),
    (S, FAR, 2),
    (S, TWO, 2),
    (S, SIDE_P, 7),
    (S, SIDE_M, 3),
    (S, TWO, 3),
    (S, SIDE, 2),
    (S, FAR, 3),
    (C, FINISH, 0),
    (S, FAR, 5),
    (S, FAR, 4),
    (S, SIDE_M, 4),
    (C, EVEN, 1),
    (C, NEAR, 1),
    (S, TWO, 7),
    (S, TWO, 6),
    (S, SIDE_P, 6),
    (S, SIDE_M, 7),
    (S, FAR, 6),
    (S, FAR, 7),
    (C, FINISH, 1),
)


class Streams:
    def __init__(self, send_sem, recv_sem):
        self.send_sem, self.recv_sem = send_sem, recv_sem
        self.number = {}
        self.started = []

    def copy(self, key, src, dst, device):
        at = self.number.setdefault(key, len(self.number))
        return pltpu.make_async_remote_copy(
            src_ref=src,
            dst_ref=dst,
            send_sem=self.send_sem.at[at],
            recv_sem=self.recv_sem.at[at],
            device_id=device,
            device_id_type=MESH,
        )

    def send(self, key, src, dst, device):
        copy = self.copy(key, src, dst, device)
        copy.start()
        self.started.append(copy)

    def arrived(self, key, dst, device):
        self.copy(key, dst, dst, device).wait_recv()


def kernel(
    values_in, columns_in, live_in, out, values, columns, live, left, right, squared, chosen, cube, in_sem, send_sem, recv_sem
):
    row, col = lax.axis_index("row"), lax.axis_index("col")
    y_lo, z = row // 4, row % 4
    y_hi, x, core = col // 8, (col // 2) % 4, col % 2

    def row_of(dy, dz):
        return ((y_lo + dy) % 2) * 4 + (z + dz + 4) % 4

    def col_of(dy, dx, dc):
        return (((y_hi + dy) % 2) * 4 + (x + dx + 4) % 4) * 2 + (core + dc) % 2

    near = {
        "y": (row_of(1, 0), col),
        "z+": (row_of(0, 1), col),
        "z-": (row_of(0, -1), col),
        "x+": (row, col_of(0, 1, 0)),
        "x-": (row, col_of(0, -1, 0)),
        "h": (row, col_of(1, 0, 0)),
        "c": (row, col_of(0, 0, 1)),
    }
    barrier = pltpu.get_barrier_semaphore()
    for device in near.values():
        pl.semaphore_signal(barrier, inc=1, device_id=device, device_id_type=MESH)

    fetches = [
        pltpu.make_async_copy(source, target, in_sem.at[at])
        for at, (source, target) in enumerate(
            [(columns_in, columns), (live_in, live)]
            + [(values_in.at[j], values.at[j]) for j in range(ROWS)]
        )
    ]
    for fetch in fetches:
        fetch.start()
    for fetch in fetches[:2]:
        fetch.wait()

    heads = [
        jnp.broadcast_to(columns[0, j].astype(jnp.float32), (1, BS)) for j in range(ROWS)
    ]
    head = jnp.concatenate(
        heads + [jnp.zeros((HEAD - ROWS, BS), jnp.float32)], axis=0
    ).astype(jnp.bfloat16)
    left[col, 0:HEAD, :] = head
    right[row, 0, 0:HEAD, :] = head[:, 0:LANES]

    def masked_block(j, lanes):
        block = values[j, 0, :, lanes].astype(jnp.float32) * live[0, j].astype(jnp.float32)
        return block.astype(jnp.bfloat16)

    def build_right(h, j):
        lanes = slice(h * LANES, (h + 1) * LANES)
        right[row, h, HEAD + j * BS : HEAD + (j + 1) * BS, :] = masked_block(j, lanes)

    def build_left(j):
        left[col, HEAD + j * BS : HEAD + (j + 1) * BS, :] = masked_block(j, slice(None))

    for j in range(ROWS):
        fetches[2 + j].wait()
        build_right(0, j)
    pl.semaphore_wait(barrier, len(near))

    streams = Streams(send_sem, recv_sem)

    def piece(buffer, unit, at):
        if buffer is left:
            if at == 0:
                return left.at[unit, pl.ds(0, HEAD + LEFT_PIECE)]
            return left.at[unit, pl.ds(HEAD + at * LEFT_PIECE, LEFT_PIECE)]
        h, j = at // ROWS, at % ROWS
        if buffer is squared:
            return squared.at[unit, h, pl.ds(j * BS, BS)]
        if at == 0:
            return right.at[unit, 0, pl.ds(0, HEAD + BS)]
        return right.at[unit, h, pl.ds(HEAD + j * BS, BS)]

    def send(name, buffer, unit, j, way):
        ref = piece(buffer, unit, j)
        streams.send((name, j, way), ref, ref, near[way])

    def arrived(name, buffer, unit, j, way):
        streams.arrived((name, j, way), piece(buffer, unit, j), near[way])

    def right_step(tag, buffer, name, j):
        two, far, side_m, side_p = (PATHS[tag, k][j] for k in ("two", "far", "m", "p"))
        if name == OWN:
            if tag == R and j >= ROWS:
                build_right(1, j - ROWS)
            for way in ("z+", "z-", "y"):
                send(tag + "own", buffer, row, j, way)
        elif name == MINUS:
            arrived(tag + "own", buffer, row_of(0, -1), j, "z+")
            if two == "+":
                send(tag + "two", buffer, row_of(0, -1), j, "z+")
            if side_m == "y":
                send(tag + "sideM", buffer, row_of(0, -1), j, "y")
        elif name == PLUS:
            arrived(tag + "own", buffer, row_of(0, 1), j, "z-")
            if two == "-":
                send(tag + "two", buffer, row_of(0, 1), j, "z-")
            if side_p == "y":
                send(tag + "sideP", buffer, row_of(0, 1), j, "y")
        elif name == SIDE:
            arrived(tag + "own", buffer, row_of(1, 0), j, "y")
            if side_m == "z":
                send(tag + "sideM", buffer, row_of(1, 0), j, "z+")
            if side_p == "z":
                send(tag + "sideP", buffer, row_of(1, 0), j, "z-")
        elif name == TWO:
            arrived(tag + "two", buffer, row_of(0, 2), j, "z" + two)
            if far == "y":
                send(tag + "far", buffer, row_of(0, 2), j, "y")
        elif name == SIDE_M:
            arrived(tag + "sideM", buffer, row_of(1, -1), j, "z+" if side_m == "z" else "y")
            if far == "+":
                send(tag + "far", buffer, row_of(1, -1), j, "z+")
        elif name == SIDE_P:
            arrived(tag + "sideP", buffer, row_of(1, 1), j, "z-" if side_p == "z" else "y")
            if far == "-":
                send(tag + "far", buffer, row_of(1, 1), j, "z-")
        elif name == FAR:
            arrived(tag + "far", buffer, row_of(1, 2), j, "y" if far == "y" else "z" + far)

    built = set()

    def left_step(name, j):
        two, far = (PATHS["L", k][j] for k in ("two", "far"))
        if name in (OWN, HOP) and j not in built:
            built.add(j)
            build_left(j)
        if name == OWN:
            for way in ("x+", "x-", "c"):
                send("Lown", left, col, j, way)
        elif name == HOP:
            send("Lown", left, col, j, "h")
        elif name == MINUS:
            arrived("Lown", left, col_of(0, -1, 0), j, "x+")
            if two == "+":
                send("Ltwo", left, col_of(0, -1, 0), j, "x+")
            send("Lm", left, col_of(0, -1, 0), j, "c")
        elif name == PLUS:
            arrived("Lown", left, col_of(0, 1, 0), j, "x-")
            if two == "-":
                send("Ltwo", left, col_of(0, 1, 0), j, "x-")
            send("Lp", left, col_of(0, 1, 0), j, "c")
        elif name == SIDE:
            arrived("Lown", left, col_of(1, 0, 0), j, "h")
            for way in ("x+", "x-", "c"):
                send("Lside", left, col_of(1, 0, 0), j, way)
        elif name == SM:
            arrived("Lside", left, col_of(1, -1, 0), j, "x+")
            if far == "+":
                send("Lfar", left, col_of(1, -1, 0), j, "x+")
            send("Lsm", left, col_of(1, -1, 0), j, "c")
        elif name == SP:
            arrived("Lside", left, col_of(1, 1, 0), j, "x-")
            if far == "-":
                send("Lfar", left, col_of(1, 1, 0), j, "x-")
            send("Lsp", left, col_of(1, 1, 0), j, "c")
        elif name == TWO:
            arrived("Ltwo", left, col_of(0, 2, 0), j, "x" + two)
            send("Ltwo", left, col_of(0, 2, 0), j, "c")
        elif name == FAR:
            arrived("Lfar", left, col_of(1, 2, 0), j, "x" + far)
            send("Lfar", left, col_of(1, 2, 0), j, "c")
        elif name == END:
            arrived("Lown", left, col_of(0, 0, 1), j, "c")
            arrived("Lm", left, col_of(0, -1, 1), j, "c")
            arrived("Lp", left, col_of(0, 1, 1), j, "c")
            arrived("Lside", left, col_of(1, 0, 1), j, "c")
            arrived("Lsm", left, col_of(1, -1, 1), j, "c")
            arrived("Lsp", left, col_of(1, 1, 1), j, "c")
            arrived("Ltwo", left, col_of(0, 2, 1), j, "c")
            arrived("Lfar", left, col_of(1, 2, 1), j, "c")

    def select(buffer, first, h, i, groups):
        mine = columns[0, i].astype(jnp.float32)
        alive = (live[0, i] > 0).astype(jnp.float32)
        for slot, (r, part) in enumerate(groups):
            right_head = right[r, 0, 0:HEAD, :].astype(jnp.float32)
            own = left[2 * r + part, 0:HEAD, 0:LANES].astype(jnp.float32)[i : i + 1]
            weights = []
            for b in range(2):
                met = right_head[2 * part + b : 2 * part + b + 1]
                weights.append(
                    jnp.where((own == float(b)) & (met == mine), alive, 0.0).astype(jnp.bfloat16)
                )
            at = first + 2 * part * BS
            chosen[slot * BS : (slot + 1) * BS, :] = (
                buffer[r, h, at : at + BS, :] * weights[0]
                + buffer[r, h, at + BS : at + 2 * BS, :] * weights[1]
            )

    def product(i, groups):
        return jnp.dot(
            jnp.concatenate(
                [
                    left[2 * r + part, HEAD + i * BS : HEAD + (i + 1) * BS, :]
                    for r, part in groups
                ],
                axis=1,
            ),
            chosen[0 : len(groups) * BS, :],
            preferred_element_type=jnp.float32,
        )

    both = [(r, part) for r in range(NR) for part in range(2)]
    even = [(r, 0) for r in range(NR)]
    odd = [(r, 1) for r in range(NR)]
    odd_near = [(row_of(dy, dz), 1) for dy, dz in ((0, 0), (1, 0), (0, -1), (0, 1))]
    odd_far = [(row_of(dy, dz), 1) for dy, dz in ((0, 2), (1, -1), (1, 1), (1, 2))]

    def square(h, i):
        select(right, HEAD, h, i, both)
        squared[row, h, i * BS : (i + 1) * BS, :] = product(i, both).astype(jnp.bfloat16)

    def cube_even(h):
        for i in range(ROWS):
            select(squared, 0, h, i, even)
            cube[h, i * BS : (i + 1) * BS, :] = product(i, even)

    def cube_near(h):
        for i in range(ROWS):
            select(squared, 0, h, i, odd_near)
            cube[h, i * BS : (i + 1) * BS, :] += product(i, odd_near)

    def finish(h):
        groups = odd_far if h == HALVES - 1 else odd
        lanes = slice(h * LANES, (h + 1) * LANES)
        for i in range(ROWS):
            select(squared, 0, h, i, groups)
            cube_part = cube[h, i * BS : (i + 1) * BS, :] + product(i, groups)
            masked = left[col, HEAD + i * BS : HEAD + (i + 1) * BS, lanes].astype(jnp.float32)
            out[i, 0, :, lanes] = (1.5 * masked - 0.5 * cube_part).astype(jnp.bfloat16)

    for tag, name, j in ORDER:
        if tag == R:
            right_step(tag, right, name, j)
        elif tag == S:
            right_step(tag, squared, name, j)
        elif tag == L:
            left_step(name, j)
        elif name == SQUARE:
            square(j // ROWS, j % ROWS)
        elif name == EVEN:
            cube_even(j)
        elif name == NEAR:
            cube_near(j)
        else:
            finish(j)
    for copy in streams.started:
        copy.wait_send()


COPIES = 15 * LEFT_PIECES + (7 + 7) * HALVES * ROWS


def body(block_values, block_columns, block_live):
    return pl.pallas_call(
        kernel,
        name="sign_step",
        out_shape=jax.ShapeDtypeStruct(block_values.shape, jnp.bfloat16),
        in_specs=[
            pl.BlockSpec(memory_space=pltpu.HBM),
            pl.BlockSpec(memory_space=pltpu.HBM),
            pl.BlockSpec(memory_space=pltpu.HBM),
        ],
        out_specs=pl.BlockSpec(memory_space=pltpu.VMEM),
        scratch_shapes=[
            pltpu.VMEM(block_values.shape, jnp.bfloat16),
            pltpu.SMEM((1, ROWS), jnp.int32),
            pltpu.SMEM((1, ROWS), jnp.int32),
            pltpu.VMEM((NC, HEAD + ROWS * BS, BS), jnp.bfloat16),
            pltpu.VMEM((NR, HALVES, HEAD + ROWS * BS, LANES), jnp.bfloat16),
            pltpu.VMEM((NR, HALVES, ROWS * BS, LANES), jnp.bfloat16),
            pltpu.VMEM((NC * BS, LANES), jnp.bfloat16),
            pltpu.VMEM((HALVES, ROWS * BS, LANES), jnp.float32),
            pltpu.SemaphoreType.DMA((2 + ROWS,)),
            pltpu.SemaphoreType.DMA((COPIES,)),
            pltpu.SemaphoreType.DMA((COPIES,)),
        ],
        compiler_params=pltpu.CompilerParams(
            collective_id=0, has_side_effects=True, vmem_limit_bytes=28 * 1024 * 1024
        ),
    )(block_values, block_columns.T, block_live.T)


def solution(mesh):
    return jax.shard_map(
        body,
        mesh=mesh,
        in_specs=(P("row", "col", None, None), P("row", "col"), P("row", "col")),
        out_specs=P("row", "col", None, None),
        check_vma=False,
    )
```
